32 devices in a mesh: gx: 16 (over z, y, x), gy: 2 (over core).
Axes of the slice: x: 2, y: 2, z: 4, core: 2. Of those that a mesh axis runs over, the one named last changes fastest.
Arguments:
- snapshot: bfloat16 [3, 128, 32, 1024], P(None, 'gx', 'gy'), may hold values from -6 to 6
- basis: bfloat16 [3, 16, 4, 128, 512], P(None, 'gx', 'gy'), may hold values from -3000 to 3000
- taps: bfloat16 [3, 17], replicated, may hold values from 0.099609375 to 1
Outputs:
- new_modes: bfloat16 [3, 16, 4, 128, 512], P(None, 'gx', 'gy')
- new_mode: float32 [3, 16, 4, 128], P(None, 'gx', 'gy')
- factor: float32 [513, 513], replicated
The draws below stay inside these ranges and needn't reach their ends.
All inputs are finite; a program needn't handle non-finite values.
Results may differ from the reference program's by a relative error of at most 0.0012.
The reference program's roundings to bfloat16 on the way (of `filtered` and `stack`) count: a program that leaves them out, or rounds other values in their place, can miss the bound.
Values sent between devices are 32-bit elements; how exact they have to be, the bound alone decides.
No kernel may reach another device: no remote copies, remote signals or barrier semaphores. Data moves between devices by JAX's collectives and lax.ppermute only.
A program may use at most 64 MiB of HBM per device.

```python
import math
import jax
import jax.numpy as jnp
from jax import lax

K = 512
STRIDE = 8
TAPS = 17
NZ = 1024
FZ = 128
NX = 128
NY = 32
NFX = 16
NFY = 4


def draw_basis(key, part):
    key_base = jax.random.fold_in(key, 11)
    key_rows = jax.random.fold_in(key, 12)
    key_cols = jax.random.fold_in(key, 13)
    key_pair = jax.random.fold_in(key, 14)
    key_mixing = jax.random.fold_in(key, 15)
    total = 3 * NFX * NFY * FZ
    base = jax.random.normal(key_base, (total, K), jnp.float32)
    mixing = jnp.eye(K, dtype=jnp.float32) + 0.6 * jax.random.normal(key_mixing, (K, K), jnp.float32) / math.sqrt(K)
    mixed = jnp.dot(base, mixing, precision=lax.Precision.HIGHEST)
    row_scale = jnp.exp(jax.random.uniform(key_rows, (total, 1), jnp.float32, 0.0, math.log(10.0)))
    col_scale = jnp.exp(jax.random.uniform(key_cols, (1, K), jnp.float32, 0.0, math.log(10.0)))
    slab = jnp.arange(total, dtype=jnp.int32) // (NFY * FZ) % NFX
    owner = jax.random.permutation(key_pair, NFX)
    column_slab = owner[jnp.arange(K, dtype=jnp.int32) * NFX // K]
    spike = jnp.where(slab[:, None] == column_slab[None, :], 4.0, 1.0)
    values = mixed * spike
    values = values * row_scale * col_scale
    return values.reshape(3, NFX, NFY, FZ, K).astype(jnp.bfloat16)


def shard_levels(key, shape, cuts, smallest, largest):
    factor_of = 1.0
    for dim, shards_of in cuts:
        steps = jax.random.uniform(jax.random.fold_in(jax.random.fold_in(key, 6), dim), (shards_of,), jnp.float32, smallest / len(cuts), largest / len(cuts))
        factor_of = factor_of * jnp.repeat(jnp.exp(steps), shape[dim] // shards_of).reshape((-1,) + (1,) * (len(shape) - 1 - dim))
    return factor_of


def normal_values(own_key, shape, scale, limit, cuts=(), held_as=jnp.bfloat16):
    level = shard_levels(own_key, shape, cuts, -0.22, 0.18) if cuts else 1.0
    values = jax.random.normal(own_key, shape, jnp.float32) * scale * level
    return jnp.minimum(jnp.maximum(values, -limit), limit).astype(held_as)


def setup_inputs(seed: int = 0) -> dict:
    key_list = jax.random.split(jax.random.key(seed), 4)
    return {
        "snapshot": normal_values(key_list[0], (3, NX, NY, NZ), 1.0, 6.0, ((1, 16), (2, 2))),
        "basis": draw_basis(jax.random.fold_in(key_list[3], 71), 0),
        "taps": jnp.clip(jax.random.uniform(key_list[2], (3, TAPS), jnp.float32, 0.099609375, 1.0), 0.099609375, 1.0).astype(jnp.bfloat16),
    }


def band(taps_row, length, out_len, shift, wrap):
    rows = jnp.arange(length, dtype=jnp.int32)[:, None]
    cols = jnp.arange(out_len, dtype=jnp.int32)[None, :]
    lag = rows - STRIDE * cols + shift
    if wrap:
        lag = lag % length
    hits = lag[:, :, None] == jnp.arange(2 * STRIDE + 1, dtype=jnp.int32)[None, None, :]
    return jnp.sum(jnp.where(hits, taps_row[None, None, :], jnp.zeros((), taps_row.dtype)), axis=-1).astype(taps_row.dtype)

def reference(snapshot, basis, taps):
    comps, cells_x, cells_y, cells_z = snapshot.shape
    matrix_z = band(taps[2], cells_z, cells_z // STRIDE, STRIDE, True)
    along_z = jnp.dot(snapshot.reshape(-1, cells_z).astype(jnp.float32), matrix_z.astype(jnp.float32), preferred_element_type=jnp.float32)
    along_z = along_z.reshape(comps, cells_x, cells_y, cells_z // STRIDE)
    matrix_y = band(taps[1], cells_y, cells_y // STRIDE, STRIDE, False).astype(jnp.float32)
    along_y = jnp.einsum('cxyz,yf->cxfz', along_z, matrix_y, precision=lax.Precision.HIGHEST)
    matrix_x = band(taps[0], cells_x, cells_x // STRIDE, STRIDE, True).astype(jnp.float32)
    along_x = jnp.einsum('cxyz,xf->cfyz', along_y, matrix_x, precision=lax.Precision.HIGHEST)
    filtered = along_x.astype(jnp.bfloat16).reshape(-1)
    modes = basis.shape[-1]
    stack = jnp.concatenate([basis.reshape(-1, modes), filtered[:, None]], axis=1)
    total = stack.shape[0]
    gram = jnp.einsum('rk,rj->kj', stack.astype(jnp.float32), stack.astype(jnp.float32), preferred_element_type=jnp.float32) / total
    lower = jnp.linalg.cholesky(gram)
    solved = lax.linalg.triangular_solve(lower, stack.astype(jnp.float32), left_side=False, lower=True, transpose_a=True)
    new_modes = solved[:, :modes].astype(jnp.bfloat16).reshape(basis.shape)
    new_mode = solved[:, modes].reshape(basis.shape[:-1])
    return (new_modes, new_mode, lower.T)
```

```python
import jax
import jax.numpy as jnp
from jax import lax
from jax.experimental import pallas as pl
from jax.experimental.pallas import tpu as pltpu
from jax.sharding import PartitionSpec as P

STRIDE = 8
TILE = 128
PIVOTS = 32
F32 = jnp.float32
BF16 = jnp.bfloat16
HIGHEST = lax.Precision.HIGHEST


def padded(block, sides, width, periodic):
    for axis, dim in sides:
        count = lax.axis_size(axis)
        forward = [(i, i + 1) for i in range(count - 1)]
        if periodic:
            forward.append((count - 1, 0))
        backward = [(target, source) for source, target in forward]
        low = lax.ppermute(
            lax.slice_in_dim(block, block.shape[dim] - width, None, axis=dim), axis, forward
        )
        high = lax.ppermute(lax.slice_in_dim(block, 0, width, axis=dim), axis, backward)
        block = jnp.concatenate([low, block, high], axis=dim)
    return block


def band(taps_row, length, out_len, shift, wrap):
    rows = jnp.arange(length, dtype=jnp.int32)[:, None]
    cols = jnp.arange(out_len, dtype=jnp.int32)[None, :]
    lag = rows - STRIDE * cols + shift
    if wrap:
        lag = lag % length
    hits = lag[:, :, None] == jnp.arange(2 * STRIDE + 1, dtype=jnp.int32)[None, None, :]
    return jnp.sum(jnp.where(hits, taps_row[None, None, :], jnp.zeros((), taps_row.dtype)), axis=-1)


def hops(axes):
    found = []
    for axis in axes:
        size = lax.axis_size(axis)
        if size & (size - 1):
            return None
        bit = 1
        while bit < size:
            pairs = [(i, i ^ bit) for i in range(size)]
            upper = (lax.axis_index(axis) & bit) != 0
            found.append((axis, pairs, upper))
            bit *= 2
    return found


def total_of(block, axes):
    exchanges = hops(axes)
    if exchanges is None:
        return lax.psum(block, axes)
    halved = []
    for axis, pairs, upper in exchanges:
        rows = block.shape[0]
        if rows % 16 == 0:
            low, high = block[: rows // 2], block[rows // 2 :]
            sent = jnp.where(upper, low, high)
            kept = jnp.where(upper, high, low)
            block = kept + lax.ppermute(sent, axis, pairs)
            halved.append((axis, pairs, upper))
        else:
            block = block + lax.ppermute(block, axis, pairs)
    for axis, pairs, upper in reversed(halved):
        other = lax.ppermute(block, axis, pairs)
        block = jnp.concatenate(
            [jnp.where(upper, other, block), jnp.where(upper, block, other)], axis=0
        )
    return block


def small_total(block, axes):
    exchanges = hops(axes)
    if exchanges is None:
        return lax.psum(block, axes)
    for axis, pairs, _ in exchanges:
        block = block + lax.ppermute(block, axis, pairs)
    return block


def contract_rows(a, b, precision=None):
    return lax.dot_general(
        a, b, (((0,), (0,)), ((), ())), precision=precision, preferred_element_type=F32
    )


def contract_lanes(a, b, precision=None):
    return lax.dot_general(
        a, b, (((1,), (1,)), ((), ())), precision=precision, preferred_element_type=F32
    )


def gram_kernel(rows_ref, out_ref):
    modes = rows_ref.shape[1]
    at = 0
    for p in range(modes // TILE):
        left = rows_ref[:, TILE * p : TILE * (p + 1)]
        part = contract_rows(left, rows_ref[:, TILE * p :])
        for c in range(modes // TILE - p):
            out_ref[at : at + TILE, :] = part[:, TILE * c : TILE * (c + 1)]
            at += TILE


def local_gram(rows):
    count, modes = rows.shape
    chunks = modes // TILE
    blocks = chunks * (chunks + 1) // 2
    return pl.pallas_call(
        gram_kernel,
        out_shape=jax.ShapeDtypeStruct((blocks * TILE, TILE), F32),
        cost_estimate=pl.CostEstimate(
            flops=2 * count * modes * modes, bytes_accessed=4 * blocks * TILE * TILE, transcendentals=0
        ),
        name="gram",
    )(rows)


def factor_blocks(work, scaled, upper):
    modes = work.shape[0]
    chunks = modes // TILE
    groups = PIVOTS // 8
    lane = lax.broadcasted_iota(jnp.int32, (8, TILE), 1)
    row = lax.broadcasted_iota(jnp.int32, (8, TILE), 0)
    scale_blocks = []
    for p in range(chunks):
        base = p * TILE
        for j in range(TILE // PIVOTS):
            first = PIVOTS * j
            top = base + first
            rows = [
                [work[top + 8 * g : top + 8 * g + 8, TILE * c : TILE * (c + 1)] for c in range(chunks)]
                for g in range(groups)
            ]
            cols = [
                [
                    jnp.broadcast_to(rows[g][p][:, first + k : first + k + 1], (8, TILE))
                    if g >= k // 8
                    else None
                    for g in range(groups)
                ]
                for k in range(PIVOTS)
            ]
            unit = [jnp.where(lane == first + 8 * g + row, 1.0, 0.0).astype(F32) for g in range(groups)]
            inverse = [jnp.zeros((8, TILE), F32) for _ in range(groups)]
            scale = [jnp.zeros((8, TILE), F32) for _ in range(groups)]
            for k in range(PIVOTS):
                own, sub = k // 8, k % 8
                pivot = cols[k][own][sub : sub + 1, :]
                recip = 1.0 / pivot
                inverse[own] = jnp.where(row == sub, recip, inverse[own])
                scale[own] = jnp.where(row == sub, lax.rsqrt(pivot), scale[own])
                mult = {g: cols[k][g] * recip for g in range(own, groups)}
                for later in range(k + 1, PIVOTS):
                    factor = cols[k][later // 8][later % 8 : later % 8 + 1, :]
                    for g in range(later // 8, groups):
                        cols[later][g] = cols[later][g] - mult[g] * factor
                mult[own] = jnp.where(row > sub, mult[own], 0.0)
                for c in range(chunks):
                    pivot_row = rows[own][c][sub : sub + 1, :]
                    for g in range(own, groups):
                        rows[g][c] = rows[g][c] - mult[g] * pivot_row
                pivot_row = unit[own][sub : sub + 1, :]
                for g in range(own, groups):
                    unit[g] = unit[g] - mult[g] * pivot_row
            inside = (lane >= first) & (lane < first + PIVOTS)
            for g in range(groups):
                where = slice(top + 8 * g, top + 8 * g + 8)
                for c in range(chunks):
                    cut = slice(TILE * c, TILE * (c + 1))
                    if c < p:
                        upper[where, cut] = jnp.zeros((8, TILE), F32)
                    elif c == p:
                        upper[where, cut] = jnp.where(
                            lane >= first + 8 * g + row, rows[g][c] * scale[g], 0.0
                        )
                    else:
                        upper[where, cut] = rows[g][c] * scale[g]
                    if c >= p:
                        scaled[first + 8 * g : first + 8 * g + 8, cut] = rows[g][c] * inverse[g]
                    work[where, cut] = jnp.where(inside, unit[g], rows[g][c]) if c == p else rows[g][c]
                scale_blocks.append(scale[g])
            end = first + PIVOTS
            if end < TILE:
                change = contract_rows(
                    scaled[first:end, base : base + TILE], work[top : top + PIVOTS, :], HIGHEST
                )
                wide = lax.broadcasted_iota(jnp.int32, (TILE - end, TILE), 1)
                for c in range(chunks):
                    cut = slice(TILE * c, TILE * (c + 1))
                    old = work[base + end : base + TILE, cut]
                    if c == p:
                        old = jnp.where((wide >= first) & (wide < end), 0.0, old)
                    work[base + end : base + TILE, cut] = old - change[end:, cut]
        block_lane = lax.broadcasted_iota(jnp.int32, (TILE, TILE), 1)
        block_row = lax.broadcasted_iota(jnp.int32, (TILE, TILE), 0)
        own = slice(base, base + TILE)
        work[own, own] = jnp.where(block_lane <= block_row, work[own, own], 0.0)
        for i in range(p + 1, chunks):
            below = slice(TILE * i, TILE * (i + 1))
            left = scaled[:, below]
            inverse_part = contract_rows(left, work[own, : base + TILE], HIGHEST)
            if p:
                work[below, :base] = work[below, :base] - inverse_part[:, :base]
            work[below, own] = -inverse_part[:, base:]
            gram_part = contract_rows(left, work[own, TILE * i :], HIGHEST)
            work[below, TILE * i :] = work[below, TILE * i :] - gram_part
    return scale_blocks


def solve_kernel(
    total_ref, cross_ref, fresh_ref, rows_ref, modes_ref, mode_ref, factor_ref, work, scaled, *, total
):
    modes = work.shape[0]
    chunks = modes // TILE
    at = 0
    for p in range(chunks):
        for c in range(p, chunks):
            work[TILE * p : TILE * (p + 1), TILE * c : TILE * (c + 1)] = (
                total_ref[at : at + TILE, :] * (1.0 / total)
            )
            at += TILE
    scales = factor_blocks(work, scaled, factor_ref)
    for g, scale in enumerate(scales):
        where = slice(8 * g, 8 * g + 8)
        for c in range(8 * g // TILE + 1):
            work[where, TILE * c : TILE * (c + 1)] = work[where, TILE * c : TILE * (c + 1)] * scale
    cross = [cross_ref[c : c + 1, :] * (1.0 / total) for c in range(chunks)]
    square = cross_ref[chunks : chunks + 1, :] * (1.0 / total)
    projected = []
    for p in range(chunks):
        own = slice(TILE * p, TILE * (p + 1))
        width = TILE * (p + 1)
        known = work[own, :width]
        first = known.astype(BF16)
        second = (known - first.astype(F32)).astype(BF16)
        left = rows_ref[:, :width]
        solved = contract_lanes(left, first) + contract_lanes(left, second)
        modes_ref[:, own] = solved.astype(BF16)
        line = jnp.concatenate(cross[: p + 1], axis=1)
        projected.append(contract_lanes(jnp.broadcast_to(line, (8, width)), known, HIGHEST))
        column = sum(known[:, TILE * c : TILE * (c + 1)] * cross[c] for c in range(p + 1))
        factor_ref[own, modes : modes + 1] = jnp.sum(column, axis=1, keepdims=True)
    norm = sum(jnp.sum(part * part, axis=1, keepdims=True) for part in projected)
    gap = square[:, :1] - norm[:1, :]
    last = jnp.sqrt(gap)
    share = jnp.zeros((8, modes), F32)
    back = []
    for c in range(chunks):
        own = slice(TILE * c, TILE * (c + 1))
        part = jnp.zeros((8, TILE), F32)
        for p in range(c, chunks):
            part = part + jnp.dot(
                projected[p],
                work[TILE * p : TILE * (p + 1), own],
                precision=HIGHEST,
                preferred_element_type=F32,
            )
        back.append(part)
    share = jnp.concatenate(back, axis=1)
    first = share.astype(BF16)
    second = (share - first.astype(F32)).astype(BF16)
    covered = contract_lanes(first, rows_ref[...]) + contract_lanes(second, rows_ref[...])
    mode_ref[...] = (fresh_ref[...] - covered[:1, :]) / last
    factor_ref[modes : modes + 1, :modes] = jnp.zeros((1, modes), F32)
    factor_ref[modes : modes + 1, modes : modes + 1] = last


def solve(total_gram, total_cross, fresh, rows, total):
    count, modes = rows.shape
    return pl.pallas_call(
        lambda *refs: solve_kernel(*refs, total=total),
        out_shape=(
            jax.ShapeDtypeStruct((count, modes), BF16),
            jax.ShapeDtypeStruct((1, count), F32),
            jax.ShapeDtypeStruct((modes + 1, modes + 1), F32),
        ),
        scratch_shapes=[pltpu.VMEM((modes, modes), F32), pltpu.VMEM((TILE, modes), F32)],
        cost_estimate=pl.CostEstimate(
            flops=4 * count * modes * modes, bytes_accessed=8 * modes * modes, transcendentals=modes
        ),
        name="solve",
    )(total_gram, total_cross, fresh, rows)


def local(snapshot, basis, taps):
    comps, cells_x, cells_y, cells_z = snapshot.shape
    modes = basis.shape[-1]
    axes = ("gy", "gx")
    flat_rows = basis.reshape(-1, modes)
    total = flat_rows.shape[0] * lax.axis_size("gx") * lax.axis_size("gy")
    gram = total_of(local_gram(flat_rows), axes)
    matrix_z = band(taps[2], cells_z, cells_z // STRIDE, STRIDE, True)
    along_z = jnp.dot(snapshot.reshape(-1, cells_z), matrix_z, preferred_element_type=F32)
    along_z = along_z.reshape(comps, cells_x, cells_y, cells_z // STRIDE)
    padded_y = padded(along_z, (("gy", 2),), STRIDE, False)
    matrix_y = band(taps[1], cells_y + 2 * STRIDE, cells_y // STRIDE, 0, False).astype(F32)
    along_y = jnp.einsum("cxyz,yf->cxfz", padded_y, matrix_y, precision=HIGHEST)
    padded_x = padded(along_y, (("gx", 1),), STRIDE, True)
    matrix_x = band(taps[0], cells_x + 2 * STRIDE, cells_x // STRIDE, 0, False).astype(F32)
    along_x = jnp.einsum("cxyz,xf->cfyz", padded_x, matrix_x, precision=HIGHEST)
    fresh = lax.reduce_precision(along_x, exponent_bits=8, mantissa_bits=7).reshape(-1)
    filtered = fresh.astype(BF16)
    cross = jnp.einsum("rk,r->k", flat_rows, filtered, preferred_element_type=F32)
    square = jnp.full((TILE,), jnp.sum(fresh * fresh), F32)
    sums = jnp.concatenate([cross, square]).reshape(-1, TILE)
    sums = small_total(sums, axes)
    new_modes, new_mode, factor = solve(gram, sums, fresh.reshape(1, -1), flat_rows, total)
    return (new_modes.reshape(basis.shape), new_mode.reshape(basis.shape[:-1]), factor)


def solution(mesh):
    in_specs = (P(None, "gx", "gy", None), P(None, "gx", "gy", None, None), P())
    out_specs = (P(None, "gx", "gy", None, None), P(None, "gx", "gy", None), P())
    return jax.shard_map(local, mesh=mesh, in_specs=in_specs, out_specs=out_specs, check_vma=False)
```

```python
import jax
import jax.numpy as jnp
from jax import lax
from jax.experimental import pallas as pl
from jax.experimental.pallas import tpu as pltpu
from jax.sharding import PartitionSpec as P

STRIDE = 8
TILE = 128
PIVOTS = 32
F32 = jnp.float32
BF16 = jnp.bfloat16
HIGHEST = lax.Precision.HIGHEST


def swap(block, axis, step):
    return lax.ppermute(block, axis, [(i, i ^ step) for i in range(lax.axis_size(axis))])


def bit_groups(size):
    groups, bit = [], 1
    while bit < size:
        groups.append((bit, 2 * bit, 3 * bit) if 4 * bit <= size else (bit,))
        bit *= 4 if 4 * bit <= size else 2
    return groups


def contract_rows(a, b, precision=None):
    return lax.dot_general(
        a, b, (((0,), (0,)), ((), ())), precision=precision, preferred_element_type=F32
    )


def contract_lanes(a, b, precision=None):
    return lax.dot_general(
        a, b, (((1,), (1,)), ((), ())), precision=precision, preferred_element_type=F32
    )


def upper_blocks(chunks):
    return [(p, c) for p in range(chunks) for c in range(p, chunks)]


def gram_kernel(side_ref, rows_ref, out_ref):
    blocks = upper_blocks(rows_ref.shape[1] // TILE)
    half = len(blocks) // 2
    for side in range(2):

        @pl.when(side_ref[0] == side)
        def _():
            mine = blocks[half * side : half * (side + 1)]
            for p in sorted({p for p, _ in mine}):
                cols = [c for q, c in mine if q == p]
                part = contract_rows(
                    rows_ref[:, TILE * p : TILE * (p + 1)],
                    rows_ref[:, TILE * cols[0] : TILE * (cols[-1] + 1)],
                )
                for c in cols:
                    at = TILE * mine.index((p, c))
                    out_ref[at : at + TILE, :] = part[:, TILE * (c - cols[0]) : TILE * (c - cols[0] + 1)]


def half_gram(side, rows):
    count, modes = rows.shape
    height = TILE * len(upper_blocks(modes // TILE)) // 2
    return pl.pallas_call(
        gram_kernel,
        out_shape=jax.ShapeDtypeStruct((height, TILE), F32),
        in_specs=[pl.BlockSpec(memory_space=pltpu.SMEM), pl.BlockSpec(memory_space=pltpu.VMEM)],
        cost_estimate=pl.CostEstimate(
            flops=2 * count * height * TILE, bytes_accessed=4 * height * TILE, transcendentals=0
        ),
        name="gram",
    )(side.reshape(1), rows)


def weights(taps_ref, direction, lag):
    found = jnp.zeros(lag.shape, F32)
    for tap in range(2 * STRIDE + 1):
        found = jnp.where(lag == tap, taps_ref[direction, tap], found)
    return found


def filter_kernel(taps_ref, cells_ref, out_ref, band, *, comps, cells_x, cells_y):
    depth, points = band.shape
    height = out_ref.shape[0]
    step = TILE // STRIDE
    z = lax.broadcasted_iota(jnp.int32, (TILE, points), 0)
    p = lax.broadcasted_iota(jnp.int32, (TILE, points), 1)
    for block in range(depth // TILE):
        lag = z + TILE * block - STRIDE * p + STRIDE
        lag = jnp.where(lag < 0, lag + depth, lag)
        lag = jnp.where(lag >= depth, lag - depth, lag)
        if block == 0:
            pattern = weights(taps_ref, 2, lag)
            band[:TILE, :] = pattern.astype(BF16)
        else:
            band[TILE * block : TILE * (block + 1), :] = pltpu.roll(pattern, step * block, 1).astype(BF16)
    along_z = jnp.dot(cells_ref[...], band[...], preferred_element_type=F32)
    count = cells_ref.shape[0]
    wide_r = cells_x // STRIDE + 2
    out = lax.broadcasted_iota(jnp.int32, (height, count), 0)
    cell = lax.broadcasted_iota(jnp.int32, (height, count), 1)
    comp, r, q = out % comps, out // comps % wide_r, out // (comps * wide_r)
    x, y = cell // cells_y % cells_x, cell % cells_y
    weight = weights(taps_ref, 0, x - STRIDE * (r - 1) + STRIDE)
    weight = weight * weights(taps_ref, 1, y - STRIDE * (q - 1) + STRIDE)
    weight = jnp.where(cell // (cells_x * cells_y) == comp, weight, 0.0)
    out_ref[...] = jnp.dot(weight, along_z, precision=HIGHEST, preferred_element_type=F32)


def local_filter(taps, snapshot):
    comps, cells_x, cells_y, cells_z = snapshot.shape
    wide_r, wide_q = cells_x // STRIDE + 2, cells_y // STRIDE + 2
    points = cells_z // STRIDE
    used = comps * wide_r * wide_q
    height = -(-used // 8) * 8
    cells = snapshot.reshape(-1, cells_z)
    sums = pl.pallas_call(
        lambda *refs: filter_kernel(*refs, comps=comps, cells_x=cells_x, cells_y=cells_y),
        out_shape=jax.ShapeDtypeStruct((height, points), F32),
        in_specs=[pl.BlockSpec(memory_space=pltpu.SMEM), pl.BlockSpec(memory_space=pltpu.VMEM)],
        scratch_shapes=[pltpu.VMEM((cells_z, points), BF16)],
        cost_estimate=pl.CostEstimate(
            flops=4 * cells.size * points, bytes_accessed=2 * cells.size, transcendentals=0
        ),
        name="filter",
    )(taps.astype(F32), cells)
    return sums[:used].reshape(wide_q, wide_r, comps, points)


def fold_neighbours(parts, axis, periodic):
    count = lax.axis_size(axis)
    own = parts[1:-1]
    if count == 2 and not periodic:
        upper = lax.axis_index(axis) == 1
        other = swap(jnp.where(upper, parts[0], parts[-1]), axis, 1)
        zero = jnp.zeros_like(other)
        low, high = jnp.where(upper, other, zero), jnp.where(upper, zero, other)
    else:
        forward = [(i, i + 1) for i in range(count - 1)] + ([(count - 1, 0)] if periodic else [])
        low = lax.ppermute(parts[-1], axis, forward)
        high = lax.ppermute(parts[0], axis, [(target, source) for source, target in forward])
    inner = own.shape[0]
    if inner == 1:
        return own + (low + high)[None]
    return jnp.concatenate([(own[0] + low)[None], own[1:-1], (own[-1] + high)[None]])


def cross_kernel(fresh_ref, rows_ref, out_ref):
    lines, points = fresh_ref.shape
    modes = rows_ref.shape[1]
    total = jnp.zeros((8, modes), F32)
    square = jnp.zeros((1, 1), F32)
    for i in range(lines):
        line = fresh_ref[i : i + 1, :]
        square = square + jnp.sum(line * line, axis=1, keepdims=True)
        left = jnp.broadcast_to(line, (8, points)).astype(BF16)
        total = total + jnp.dot(
            left, rows_ref[points * i : points * (i + 1), :], preferred_element_type=F32
        )
    out_ref[...] = jnp.zeros(out_ref.shape, F32)
    for c in range(modes // TILE):
        out_ref[c : c + 1, :] = total[:1, TILE * c : TILE * (c + 1)]
    out_ref[modes // TILE : modes // TILE + 1, :] = jnp.broadcast_to(square, (1, TILE))


def local_cross(fresh, rows):
    height = -(-(rows.shape[1] // TILE + 1) // 8) * 8
    return pl.pallas_call(
        cross_kernel,
        out_shape=jax.ShapeDtypeStruct((height, TILE), F32),
        cost_estimate=pl.CostEstimate(flops=16 * rows.size, bytes_accessed=2 * rows.size, transcendentals=0),
        name="cross",
    )(fresh, rows)


def factor_blocks(work, scaled, upper):
    modes = work.shape[0]
    chunks = modes // TILE
    groups = PIVOTS // 8
    lane = lax.broadcasted_iota(jnp.int32, (8, TILE), 1)
    row = lax.broadcasted_iota(jnp.int32, (8, TILE), 0)
    scale_blocks = []
    for p in range(chunks):
        base = p * TILE
        for j in range(TILE // PIVOTS):
            first = PIVOTS * j
            top = base + first
            rows = [
                [work[top + 8 * g : top + 8 * g + 8, TILE * c : TILE * (c + 1)] for c in range(chunks)]
                for g in range(groups)
            ]
            cols = [
                [
                    jnp.broadcast_to(rows[g][p][:, first + k : first + k + 1], (8, TILE))
                    if g >= k // 8
                    else None
                    for g in range(groups)
                ]
                for k in range(PIVOTS)
            ]
            unit = [jnp.where(lane == first + 8 * g + row, 1.0, 0.0).astype(F32) for g in range(groups)]
            inverse = [jnp.zeros((8, TILE), F32) for _ in range(groups)]
            scale = [jnp.zeros((8, TILE), F32) for _ in range(groups)]
            for k in range(PIVOTS):
                own, sub = k // 8, k % 8
                pivot = cols[k][own][sub : sub + 1, :]
                recip = 1.0 / pivot
                inverse[own] = jnp.where(row == sub, recip, inverse[own])
                scale[own] = jnp.where(row == sub, lax.rsqrt(pivot), scale[own])
                mult = {g: cols[k][g] * recip for g in range(own, groups)}
                for later in range(k + 1, PIVOTS):
                    factor = cols[k][later // 8][later % 8 : later % 8 + 1, :]
                    for g in range(later // 8, groups):
                        cols[later][g] = cols[later][g] - mult[g] * factor
                mult[own] = jnp.where(row > sub, mult[own], 0.0)
                for c in range(chunks):
                    pivot_row = rows[own][c][sub : sub + 1, :]
                    for g in range(own, groups):
                        rows[g][c] = rows[g][c] - mult[g] * pivot_row
                pivot_row = unit[own][sub : sub + 1, :]
                for g in range(own, groups):
                    unit[g] = unit[g] - mult[g] * pivot_row
            inside = (lane >= first) & (lane < first + PIVOTS)
            for g in range(groups):
                where = slice(top + 8 * g, top + 8 * g + 8)
                for c in range(chunks):
                    cut = slice(TILE * c, TILE * (c + 1))
                    if c < p:
                        upper[where, cut] = jnp.zeros((8, TILE), F32)
                    elif c == p:
                        upper[where, cut] = jnp.where(
                            lane >= first + 8 * g + row, rows[g][c] * scale[g], 0.0
                        )
                    else:
                        upper[where, cut] = rows[g][c] * scale[g]
                    if c >= p:
                        scaled[first + 8 * g : first + 8 * g + 8, cut] = rows[g][c] * inverse[g]
                    work[where, cut] = jnp.where(inside, unit[g], rows[g][c]) if c == p else rows[g][c]
                scale_blocks.append(scale[g])
            end = first + PIVOTS
            if end < TILE:
                change = contract_rows(
                    scaled[first:end, base : base + TILE], work[top : top + PIVOTS, :], HIGHEST
                )
                wide = lax.broadcasted_iota(jnp.int32, (TILE - end, TILE), 1)
                for c in range(chunks):
                    cut = slice(TILE * c, TILE * (c + 1))
                    old = work[base + end : base + TILE, cut]
                    if c == p:
                        old = jnp.where((wide >= first) & (wide < end), 0.0, old)
                    work[base + end : base + TILE, cut] = old - change[end:, cut]
        block_lane = lax.broadcasted_iota(jnp.int32, (TILE, TILE), 1)
        block_row = lax.broadcasted_iota(jnp.int32, (TILE, TILE), 0)
        own = slice(base, base + TILE)
        work[own, own] = jnp.where(block_lane <= block_row, work[own, own], 0.0)
        for i in range(p + 1, chunks):
            below = slice(TILE * i, TILE * (i + 1))
            left = scaled[:, below]
            inverse_part = contract_rows(left, work[own, : base + TILE], HIGHEST)
            if p:
                work[below, :base] = work[below, :base] - inverse_part[:, :base]
            work[below, own] = -inverse_part[:, base:]
            gram_part = contract_rows(left, work[own, TILE * i :], HIGHEST)
            work[below, TILE * i :] = work[below, TILE * i :] - gram_part
    return scale_blocks


def solve_kernel(
    place_ref, mine_ref, other_ref, fresh_ref, rows_ref, modes_ref, mode_ref, factor_ref,
    work, scaled, blocks, *, total,
):
    modes = work.shape[0]
    chunks = modes // TILE
    half = blocks.shape[0] // 2
    piece = half // 4
    for part_ref, side in ((mine_ref, place_ref[0]), (other_ref, 1 - place_ref[0])):
        for step in range(4):
            at = pl.multiple_of(half * side + piece * (place_ref[1] ^ step), 8)
            blocks[pl.ds(at, piece), :] = part_ref[piece * step : piece * (step + 1), :] * (1.0 / total)
    for at, (p, c) in enumerate(upper_blocks(chunks)):
        work[TILE * p : TILE * (p + 1), TILE * c : TILE * (c + 1)] = blocks[TILE * at : TILE * (at + 1), :]
    scales = factor_blocks(work, scaled, factor_ref)
    for g, scale in enumerate(scales):
        where = slice(8 * g, 8 * g + 8)
        for c in range(8 * g // TILE + 1):
            work[where, TILE * c : TILE * (c + 1)] = work[where, TILE * c : TILE * (c + 1)] * scale
    sums = (mine_ref[half : half + chunks + 1, :] + other_ref[half : half + chunks + 1, :]) * (1.0 / total)
    cross = [sums[c : c + 1, :] for c in range(chunks)]
    square = sums[chunks : chunks + 1, :]
    projected = []
    for p in range(chunks):
        own = slice(TILE * p, TILE * (p + 1))
        width = TILE * (p + 1)
        known = work[own, :width]
        first = known.astype(BF16)
        second = (known - first.astype(F32)).astype(BF16)
        left = rows_ref[:, :width]
        solved = contract_lanes(left, first) + contract_lanes(left, second)
        modes_ref[:, own] = solved.astype(BF16)
        line = jnp.concatenate(cross[: p + 1], axis=1)
        projected.append(contract_lanes(jnp.broadcast_to(line, (8, width)), known, HIGHEST))
        column = sum(known[:, TILE * c : TILE * (c + 1)] * cross[c] for c in range(p + 1))
        factor_ref[own, modes : modes + 1] = jnp.sum(column, axis=1, keepdims=True)
    norm = sum(jnp.sum(part * part, axis=1, keepdims=True) for part in projected)
    gap = square[:, :1] - norm[:1, :]
    last = jnp.sqrt(gap)
    share = jnp.zeros((8, modes), F32)
    back = []
    for c in range(chunks):
        own = slice(TILE * c, TILE * (c + 1))
        part = jnp.zeros((8, TILE), F32)
        for p in range(c, chunks):
            part = part + jnp.dot(
                projected[p],
                work[TILE * p : TILE * (p + 1), own],
                precision=HIGHEST,
                preferred_element_type=F32,
            )
        back.append(part)
    share = jnp.concatenate(back, axis=1)
    first = share.astype(BF16)
    second = (share - first.astype(F32)).astype(BF16)
    covered = contract_lanes(first, rows_ref[...]) + contract_lanes(second, rows_ref[...])
    mode_ref[...] = (fresh_ref[...] - covered[:1, :]) / last
    factor_ref[modes : modes + 1, :modes] = jnp.zeros((1, modes), F32)
    factor_ref[modes : modes + 1, modes : modes + 1] = last


def solve(place, mine, other, fresh, rows, total):
    count, modes = rows.shape
    height = TILE * len(upper_blocks(modes // TILE))
    vmem = pl.BlockSpec(memory_space=pltpu.VMEM)
    return pl.pallas_call(
        lambda *refs: solve_kernel(*refs, total=total),
        out_shape=(
            jax.ShapeDtypeStruct((count, modes), BF16),
            jax.ShapeDtypeStruct((1, count), F32),
            jax.ShapeDtypeStruct((modes + 1, modes + 1), F32),
        ),
        in_specs=[pl.BlockSpec(memory_space=pltpu.SMEM)] + [vmem] * 4,
        scratch_shapes=[
            pltpu.VMEM((modes, modes), F32),
            pltpu.VMEM((TILE, modes), F32),
            pltpu.VMEM((height, TILE), F32),
        ],
        cost_estimate=pl.CostEstimate(
            flops=4 * count * modes * modes, bytes_accessed=8 * modes * modes, transcendentals=modes
        ),
        name="solve",
    )(place, mine, other, fresh, rows)


def local(snapshot, basis, taps):
    modes = basis.shape[-1]
    rows = basis.reshape(-1, modes)
    total = rows.shape[0] * lax.axis_size("gx") * lax.axis_size("gy")
    side = lax.axis_index("gy") & 1
    member = lax.axis_index("gx") & 3
    first, *others = bit_groups(lax.axis_size("gx"))

    away = swap(half_gram(1 - side, rows), "gy", 1)
    half = half_gram(side, rows) + away
    bit = 2
    while bit < lax.axis_size("gy"):
        half = half + swap(half, "gy", bit)
        bit *= 2
    piece = half.shape[0] // 4
    quarters = half.reshape(4, piece, TILE)
    quarter = lax.dynamic_index_in_dim(quarters, member, 0, keepdims=False)
    arrived = [
        swap(lax.dynamic_index_in_dim(quarters, member ^ step, 0, keepdims=False), "gx", step)
        for step in first
    ]
    quarter = quarter + arrived[0] + arrived[1] + arrived[2]

    parts = fold_neighbours(local_filter(taps, snapshot), "gy", False)
    parts = fold_neighbours(jnp.swapaxes(parts, 0, 1), "gx", True)
    fresh = lax.reduce_precision(jnp.transpose(parts, (2, 0, 1, 3)), exponent_bits=8, mantissa_bits=7)
    fresh = fresh.reshape(-1, fresh.shape[-1])
    cross = local_cross(fresh, rows)
    bit = 2
    while bit < lax.axis_size("gy"):
        cross = cross + swap(cross, "gy", bit)
        bit *= 2

    block = jnp.concatenate([quarter, cross])
    for steps in others:
        block = sum([swap(block, "gx", step) for step in steps], block)
    gathered = [block] + [swap(block, "gx", step) for step in first]
    sums = sum([got[piece:] for got in gathered[1:]], block[piece:])
    mine = jnp.concatenate([got[:piece] for got in gathered] + [sums])
    other = swap(mine, "gy", 1)
    place = jnp.stack([side, member]).astype(jnp.int32)
    new_modes, new_mode, factor = solve(place, mine, other, fresh.reshape(1, -1), rows, total)
    return (new_modes.reshape(basis.shape), new_mode.reshape(basis.shape[:-1]), factor)


def solution(mesh):
    in_specs = (P(None, "gx", "gy", None), P(None, "gx", "gy", None, None), P())
    out_specs = (P(None, "gx", "gy", None, None), P(None, "gx", "gy", None), P())
    return jax.shard_map(local, mesh=mesh, in_specs=in_specs, out_specs=out_specs, check_vma=False)
```

```python
import jax
import jax.numpy as jnp
from jax import lax
from jax.experimental import pallas as pl
from jax.experimental.pallas import tpu as pltpu
from jax.sharding import PartitionSpec as P

STRIDE = 8
TILE = 128
PIVOTS = 32
F32 = jnp.float32
BF16 = jnp.bfloat16
HIGHEST = lax.Precision.HIGHEST


def swap(block, axis, step):
    return lax.ppermute(block, axis, [(i, i ^ step) for i in range(lax.axis_size(axis))])


def bit_groups(size):
    groups, bit = [], 1
    while bit < size:
        groups.append((bit, 2 * bit, 3 * bit) if 4 * bit <= size else (bit,))
        bit *= 4 if 4 * bit <= size else 2
    return groups


def contract_rows(a, b, precision=None):
    return lax.dot_general(
        a, b, (((0,), (0,)), ((), ())), precision=precision, preferred_element_type=F32
    )


def contract_lanes(a, b, precision=None):
    return lax.dot_general(
        a, b, (((1,), (1,)), ((), ())), precision=precision, preferred_element_type=F32
    )


def upper_blocks(chunks):
    return [(p, c) for p in range(chunks) for c in range(p, chunks)]


def gram_kernel(side_ref, rows_ref, out_ref):
    blocks = upper_blocks(rows_ref.shape[1] // TILE)
    half = len(blocks) // 2
    for side in range(2):

        @pl.when(side_ref[0] == side)
        def _():
            mine = blocks[half * side : half * (side + 1)]
            for p in sorted({p for p, _ in mine}):
                cols = [c for q, c in mine if q == p]
                part = contract_rows(
                    rows_ref[:, TILE * p : TILE * (p + 1)],
                    rows_ref[:, TILE * cols[0] : TILE * (cols[-1] + 1)],
                )
                for c in cols:
                    at = TILE * mine.index((p, c))
                    out_ref[at : at + TILE, :] = part[:, TILE * (c - cols[0]) : TILE * (c - cols[0] + 1)]


def half_gram(side, rows):
    count, modes = rows.shape
    height = TILE * len(upper_blocks(modes // TILE)) // 2
    return pl.pallas_call(
        gram_kernel,
        out_shape=jax.ShapeDtypeStruct((height, TILE), F32),
        in_specs=[pl.BlockSpec(memory_space=pltpu.SMEM), pl.BlockSpec(memory_space=pltpu.VMEM)],
        cost_estimate=pl.CostEstimate(
            flops=2 * count * height * TILE, bytes_accessed=4 * height * TILE, transcendentals=0
        ),
        compiler_params=pltpu.CompilerParams(vmem_limit_bytes=4 << 20),
        name="gram",
    )(side.reshape(1), rows)


def weights(taps_ref, direction, lag):
    line = taps_ref[...].astype(F32)[direction : direction + 1, :]
    found = jnp.zeros(lag.shape, F32)
    for tap in range(2 * STRIDE + 1):
        value = jnp.broadcast_to(line[:, tap : tap + 1], (1, lag.shape[1]))
        found = jnp.where(lag == tap, value, found)
    return found


def parted(index, size, bound):
    if size & (size - 1) == 0:
        return index >> (size.bit_length() - 1), index & (size - 1)
    scale = -(-(1 << 16) // size)
    assert all((i * scale) >> 16 == i // size for i in range(bound))
    quotient = (index * scale) >> 16
    return quotient, index - size * quotient


def filter_kernel(taps_ref, cells_ref, out_ref, band, *, comps, cells_x, cells_y):
    depth, points = band.shape
    height = out_ref.shape[0]
    z = lax.broadcasted_iota(jnp.int32, (TILE, points), 0)
    p = lax.broadcasted_iota(jnp.int32, (TILE, points), 1)
    lag = z - STRIDE * p + STRIDE
    pattern = weights(taps_ref, 2, jnp.where(lag < 0, lag + depth, lag))
    for block in range(depth // TILE):
        turned = pltpu.roll(pattern, TILE // STRIDE * block, 1) if block else pattern
        band[TILE * block : TILE * (block + 1), :] = turned.astype(BF16)
    along_z = jnp.dot(cells_ref[...], band[...], preferred_element_type=F32)
    count = cells_ref.shape[0]
    per_y = cells_y // STRIDE
    out = lax.broadcasted_iota(jnp.int32, (height, count), 0)
    cell = lax.broadcasted_iota(jnp.int32, (height, count), 1)
    slot, within = parted(out, height // 9, height)
    kind, r = parted(slot, 3, 9)
    comp, q = parted(within, per_y, height // 9)
    rest, y = parted(cell, cells_y, count)
    cell_comp, x = parted(rest, cells_x, count)
    y = y + jnp.where(kind == 1, -cells_y, jnp.where(kind == 2, cells_y, 0))
    weight = weights(taps_ref, 0, x - STRIDE * (r - 1) + STRIDE)
    weight = weight * weights(taps_ref, 1, y - STRIDE * q + STRIDE)
    weight = jnp.where(cell_comp == comp, weight, 0.0)
    out_ref[...] = jnp.dot(weight, along_z, precision=HIGHEST, preferred_element_type=F32)


def local_filter(taps, snapshot):
    comps, cells_x, cells_y, cells_z = snapshot.shape
    assert cells_x == STRIDE
    points = cells_z // STRIDE
    height = 9 * padded_rows(comps * cells_y // STRIDE)
    cells = snapshot.reshape(-1, cells_z)
    return pl.pallas_call(
        lambda *refs: filter_kernel(*refs, comps=comps, cells_x=cells_x, cells_y=cells_y),
        out_shape=jax.ShapeDtypeStruct((height, points), F32),
        scratch_shapes=[pltpu.VMEM((cells_z, points), BF16)],
        cost_estimate=pl.CostEstimate(
            flops=4 * cells.size * points, bytes_accessed=2 * cells.size, transcendentals=0
        ),
        compiler_params=pltpu.CompilerParams(vmem_limit_bytes=4 << 20),
        name="filter",
    )(taps, cells)


def padded_rows(rows):
    return -(-rows // 8) * 8


def along_slabs_y(parts):
    height = parts.shape[0] // 3
    own, up, down = parts[:height], parts[height : 2 * height], parts[2 * height :]
    count = lax.axis_size("gy")
    if count == 2:
        return own + swap(jnp.where(lax.axis_index("gy") == 1, down, up), "gy", 1)
    pairs = [(i, i + 1) for i in range(count - 1)]
    low = lax.ppermute(up, "gy", pairs)
    return own + low + lax.ppermute(down, "gy", [(j, i) for i, j in pairs])


def cross_kernel(own_ref, low_ref, high_ref, rows_ref, fresh_ref, out_ref):
    lines, points = fresh_ref.shape
    modes = rows_ref.shape[1]
    fresh = (own_ref[...] + low_ref[...] + high_ref[...]).astype(BF16).astype(F32)
    fresh_ref[...] = fresh[:lines, :]
    total = jnp.zeros((8, modes), F32)
    square = jnp.zeros((1, 1), F32)
    for i in range(lines):
        line = fresh[i : i + 1, :]
        square = square + jnp.sum(line * line, axis=1, keepdims=True)
        left = jnp.broadcast_to(line, (8, points)).astype(BF16)
        total = total + jnp.dot(
            left, rows_ref[points * i : points * (i + 1), :], preferred_element_type=F32
        )
    out_ref[...] = jnp.zeros(out_ref.shape, F32)
    for c in range(modes // TILE):
        out_ref[c : c + 1, :] = total[:1, TILE * c : TILE * (c + 1)]
    out_ref[modes // TILE : modes // TILE + 1, :] = jnp.broadcast_to(square, (1, TILE))


def local_cross(own, low, high, rows):
    points = own.shape[1]
    return pl.pallas_call(
        cross_kernel,
        out_shape=(
            jax.ShapeDtypeStruct((rows.shape[0] // points, points), F32),
            jax.ShapeDtypeStruct((padded_rows(rows.shape[1] // TILE + 1), TILE), F32),
        ),
        cost_estimate=pl.CostEstimate(flops=16 * rows.size, bytes_accessed=2 * rows.size, transcendentals=0),
        compiler_params=pltpu.CompilerParams(vmem_limit_bytes=4 << 20),
        name="cross",
    )(own, low, high, rows)


def split(value):
    parts = []
    for _ in range(3):
        parts.append(value.astype(BF16))
        value = value - parts[-1].astype(F32)
    return parts


def left_parts(value):
    a, b, c = split(value)
    return jnp.concatenate([a, a, b, b, a, c])


def right_parts(value):
    a, b, c = split(value)
    return jnp.concatenate([a, b, a, b, c, a])


def factor_blocks(work, scaled, upper):
    modes = work.shape[0]
    chunks = modes // TILE
    groups = PIVOTS // 8
    lane = lax.broadcasted_iota(jnp.int32, (8, TILE), 1)
    row = lax.broadcasted_iota(jnp.int32, (8, TILE), 0)
    scale_blocks = []
    for p in range(chunks):
        base = p * TILE
        for j in range(TILE // PIVOTS):
            first = PIVOTS * j
            top = base + first
            rows = [
                [work[top + 8 * g : top + 8 * g + 8, TILE * c : TILE * (c + 1)] for c in range(chunks)]
                for g in range(groups)
            ]
            cols = [
                [
                    jnp.broadcast_to(rows[g][p][:, first + k : first + k + 1], (8, TILE))
                    if g >= k // 8
                    else None
                    for g in range(groups)
                ]
                for k in range(PIVOTS)
            ]
            unit = [jnp.where(lane == first + 8 * g + row, 1.0, 0.0).astype(F32) for g in range(groups)]
            inverse = [jnp.zeros((8, TILE), F32) for _ in range(groups)]
            scale = [jnp.zeros((8, TILE), F32) for _ in range(groups)]
            for k in range(PIVOTS):
                own, sub = k // 8, k % 8
                pivot = cols[k][own][sub : sub + 1, :]
                recip = 1.0 / pivot
                inverse[own] = jnp.where(row == sub, recip, inverse[own])
                scale[own] = jnp.where(row == sub, lax.rsqrt(pivot), scale[own])
                mult = {g: cols[k][g] * recip for g in range(own, groups)}
                for later in range(k + 1, PIVOTS):
                    factor = cols[k][later // 8][later % 8 : later % 8 + 1, :]
                    for g in range(later // 8, groups):
                        cols[later][g] = cols[later][g] - mult[g] * factor
                mult[own] = jnp.where(row > sub, mult[own], 0.0)
                for c in range(chunks):
                    pivot_row = rows[own][c][sub : sub + 1, :]
                    for g in range(own, groups):
                        rows[g][c] = rows[g][c] - mult[g] * pivot_row
                pivot_row = unit[own][sub : sub + 1, :]
                for g in range(own, groups):
                    unit[g] = unit[g] - mult[g] * pivot_row
            inside = (lane >= first) & (lane < first + PIVOTS)
            for g in range(groups):
                where = slice(top + 8 * g, top + 8 * g + 8)
                for c in range(chunks):
                    cut = slice(TILE * c, TILE * (c + 1))
                    if c < p:
                        upper[where, cut] = jnp.zeros((8, TILE), F32)
                    elif c == p:
                        upper[where, cut] = jnp.where(
                            lane >= first + 8 * g + row, rows[g][c] * scale[g], 0.0
                        )
                    else:
                        upper[where, cut] = rows[g][c] * scale[g]
                    if c >= p:
                        scaled[first + 8 * g : first + 8 * g + 8, cut] = rows[g][c] * inverse[g]
                    work[where, cut] = jnp.where(inside, unit[g], rows[g][c]) if c == p else rows[g][c]
                scale_blocks.append(scale[g])
            end = first + PIVOTS
            if end < TILE:
                left = left_parts(jnp.concatenate([rows[g][p] * inverse[g] for g in range(groups)]))
                wide = lax.broadcasted_iota(jnp.int32, (TILE - end, TILE), 1)
                for cuts in ([p], [c for c in range(chunks) if c != p]):
                    right = [work[top : top + PIVOTS, TILE * c : TILE * (c + 1)] for c in cuts]
                    change = contract_rows(left, right_parts(jnp.concatenate(right, axis=1)))
                    for at, c in enumerate(cuts):
                        cut = slice(TILE * c, TILE * (c + 1))
                        old = work[base + end : base + TILE, cut]
                        if c == p:
                            old = jnp.where((wide >= first) & (wide < end), 0.0, old)
                        work[base + end : base + TILE, cut] = old - change[end:, TILE * at : TILE * (at + 1)]
        block_lane = lax.broadcasted_iota(jnp.int32, (TILE, TILE), 1)
        block_row = lax.broadcasted_iota(jnp.int32, (TILE, TILE), 0)
        own = slice(base, base + TILE)
        work[own, own] = jnp.where(block_lane <= block_row, work[own, own], 0.0)
        if p + 1 < chunks:
            left = left_parts(scaled[:, base + TILE :])
            right = right_parts(work[own, :])
        for i in range(p + 1, chunks):
            below = slice(TILE * i, TILE * (i + 1))
            part = left[:, TILE * (i - p - 1) : TILE * (i - p)]
            inverse_part = contract_rows(part, right[:, : base + TILE])
            if p:
                work[below, :base] = work[below, :base] - inverse_part[:, :base]
            work[below, own] = -inverse_part[:, base:]
            gram_part = contract_rows(part, right[:, TILE * i :])
            work[below, TILE * i :] = work[below, TILE * i :] - gram_part
    return scale_blocks


def factor_kernel(side_ref, member_ref, mine_ref, other_ref, inverse_ref, factor_ref, scaled, blocks, *, total):
    work = inverse_ref
    modes = work.shape[0]
    chunks = modes // TILE
    half = blocks.shape[0] // 2
    piece = half // 4
    for part_ref, side in ((mine_ref, side_ref[0]), (other_ref, 1 - side_ref[0])):
        for step in range(4):
            at = pl.multiple_of(half * side + piece * (member_ref[0] ^ step), 8)
            blocks[pl.ds(at, piece), :] = part_ref[piece * step : piece * (step + 1), :] * (1.0 / total)
    for at, (p, c) in enumerate(upper_blocks(chunks)):
        work[TILE * p : TILE * (p + 1), TILE * c : TILE * (c + 1)] = blocks[TILE * at : TILE * (at + 1), :]
    scales = factor_blocks(work, scaled, factor_ref)
    for g, scale in enumerate(scales):
        where = slice(8 * g, 8 * g + 8)
        for c in range(8 * g // TILE + 1):
            work[where, TILE * c : TILE * (c + 1)] = work[where, TILE * c : TILE * (c + 1)] * scale


def factored(side, member, mine, other, modes, total):
    height = TILE * len(upper_blocks(modes // TILE))
    smem, vmem = (pl.BlockSpec(memory_space=space) for space in (pltpu.SMEM, pltpu.VMEM))
    return pl.pallas_call(
        lambda *refs: factor_kernel(*refs, total=total),
        out_shape=(jax.ShapeDtypeStruct((modes, modes), F32),) * 2,
        in_specs=[smem, smem, vmem, vmem],
        scratch_shapes=[pltpu.VMEM((TILE, modes), F32), pltpu.VMEM((height, TILE), F32)],
        cost_estimate=pl.CostEstimate(
            flops=16 * modes**3, bytes_accessed=8 * modes * modes, transcendentals=modes
        ),
        compiler_params=pltpu.CompilerParams(vmem_limit_bytes=10 << 20),
        name="factor",
    )(side.reshape(1), member.reshape(1), mine, other)


def modes_kernel(inverse_ref, rows_ref, modes_ref):
    for p in range(inverse_ref.shape[0] // TILE):
        own = slice(TILE * p, TILE * (p + 1))
        width = TILE * (p + 1)
        known = inverse_ref[own, :width]
        first = known.astype(BF16)
        second = (known - first.astype(F32)).astype(BF16)
        left = rows_ref[:, :width]
        solved = contract_lanes(left, first) + contract_lanes(left, second)
        modes_ref[:, own] = solved.astype(BF16)


def solved_modes(inverse, rows):
    count, modes = rows.shape
    return pl.pallas_call(
        modes_kernel,
        out_shape=jax.ShapeDtypeStruct((count, modes), BF16),
        cost_estimate=pl.CostEstimate(
            flops=4 * count * modes * modes, bytes_accessed=4 * modes * modes, transcendentals=0
        ),
        compiler_params=pltpu.CompilerParams(vmem_limit_bytes=8 << 20),
        name="modes",
    )(inverse, rows)


def finish_kernel(inverse_ref, upper_ref, sums_ref, fresh_ref, rows_ref, mode_ref, factor_ref, *, total):
    modes = inverse_ref.shape[0]
    chunks = modes // TILE
    sums = sums_ref[...] * (1.0 / total)
    cross = [sums[c : c + 1, :] for c in range(chunks)]
    square = sums[chunks : chunks + 1, :]
    projected = []
    for p in range(chunks):
        own = slice(TILE * p, TILE * (p + 1))
        width = TILE * (p + 1)
        known = inverse_ref[own, :width]
        line = jnp.concatenate(cross[: p + 1], axis=1)
        projected.append(contract_lanes(jnp.broadcast_to(line, (8, width)), known, HIGHEST))
        column = sum(known[:, TILE * c : TILE * (c + 1)] * cross[c] for c in range(p + 1))
        factor_ref[own, :modes] = upper_ref[own, :]
        factor_ref[own, modes : modes + 1] = jnp.sum(column, axis=1, keepdims=True)
    norm = sum(jnp.sum(part * part, axis=1, keepdims=True) for part in projected)
    last = jnp.sqrt(square[:, :1] - norm[:1, :])
    back = []
    for c in range(chunks):
        own = slice(TILE * c, TILE * (c + 1))
        part = jnp.zeros((8, TILE), F32)
        for p in range(c, chunks):
            part = part + jnp.dot(
                projected[p],
                inverse_ref[TILE * p : TILE * (p + 1), own],
                precision=HIGHEST,
                preferred_element_type=F32,
            )
        back.append(part)
    share = jnp.concatenate(back, axis=1)
    first = share.astype(BF16)
    second = (share - first.astype(F32)).astype(BF16)
    points = fresh_ref.shape[1]
    for i in range(fresh_ref.shape[0]):
        left = rows_ref[points * i : points * (i + 1), :]
        covered = contract_lanes(first, left) + contract_lanes(second, left)
        mode_ref[:, points * i : points * (i + 1)] = (fresh_ref[i : i + 1, :] - covered[:1, :]) / last
    factor_ref[modes : modes + 1, :modes] = jnp.zeros((1, modes), F32)
    factor_ref[modes : modes + 1, modes : modes + 1] = last


def finish(inverse, upper, sums, fresh, rows, total):
    count, modes = rows.shape
    return pl.pallas_call(
        lambda *refs: finish_kernel(*refs, total=total),
        out_shape=(
            jax.ShapeDtypeStruct((1, count), F32),
            jax.ShapeDtypeStruct((modes + 1, modes + 1), F32),
        ),
        cost_estimate=pl.CostEstimate(
            flops=64 * modes * modes, bytes_accessed=8 * modes * modes, transcendentals=0
        ),
        compiler_params=pltpu.CompilerParams(vmem_limit_bytes=8 << 20),
        name="finish",
    )(inverse, upper, sums, fresh, rows)


def local(snapshot, basis, taps):
    modes = basis.shape[-1]
    rows = basis.reshape(-1, modes)
    total = rows.shape[0] * lax.axis_size("gx") * lax.axis_size("gy")
    side = lax.axis_index("gy") & 1
    place = lax.axis_index("gx")
    member = place & 3
    slabs = lax.axis_size("gx")
    first, *others = bit_groups(slabs)

    parts = local_filter(taps, snapshot)
    side, parts = lax.optimization_barrier((side, parts))
    parts = along_slabs_y(parts)
    away = swap(half_gram(1 - side, rows), "gy", 1)
    half = half_gram(side, rows) + away
    bit = 2
    while bit < lax.axis_size("gy"):
        half = half + swap(half, "gy", bit)
        bit *= 2

    piece = half.shape[0] // 4
    height = parts.shape[0] // 3
    quarters = half.reshape(4, piece, TILE)

    def quarter_of(index):
        return lax.dynamic_index_in_dim(quarters, index, 0, keepdims=False)

    before, own, after = parts[:height], parts[height : 2 * height], parts[2 * height :]
    odd = (member & 1) == 1
    riders = {1: jnp.where(odd, before, after), 3: jnp.where(odd, after, before)}
    got = {}
    for step in first:
        block = quarter_of(member ^ step)
        got[step] = swap(jnp.concatenate([block, riders[step]]) if step in riders else block, "gx", step)
    quarter = sum([got[step][:piece] for step in first], quarter_of(member))
    near, far = got[1][piece:], got[3][piece:]

    if slabs == 16:
        got = {}
        for step in others[0]:
            block = jnp.concatenate([quarter, far]) if step != 8 else quarter
            got[step] = swap(block, "gx", step)
        quarter = sum([block[:piece] for block in got.values()], quarter)
        group = place >> 2
        wanted = jnp.where(member == 0, group - 1, group + 1) & 3
        outer = jnp.where((group ^ wanted) == 1, got[4][piece:], got[12][piece:])
        far = jnp.where((member == 0) | (member == 3), outer, far)
    else:
        for steps in others:
            quarter = sum([swap(quarter, "gx", step) for step in steps], quarter)
        forward = [(i, (i + 1) % slabs) for i in range(slabs)]
        near = lax.ppermute(after, "gx", forward)
        far = lax.ppermute(before, "gx", [(j, i) for i, j in forward])

    fresh, cross = local_cross(own, near, far, rows)
    block = jnp.concatenate([quarter, cross])
    gathered = [block] + [swap(block, "gx", step) for step in first]
    sums = sum([got[piece:] for got in gathered[1:]], block[piece:])
    mine = jnp.concatenate([got[:piece] for got in gathered] + [sums])
    other = swap(mine, "gy", 1)
    sums = mine[4 * piece :] + other[4 * piece :]
    bit = 2
    while bit < lax.axis_size("gy"):
        sums = sums + swap(sums, "gy", bit)
        bit *= 2
    bit = 4
    while 2 * bit < slabs:
        sums = sums + swap(sums, "gx", bit)
        bit *= 2
    inverse, upper = factored(side, member, mine, other, modes, total)
    sums, inverse = lax.optimization_barrier((sums, inverse))
    if bit < slabs:
        sums = sums + swap(sums, "gx", bit)
    new_modes = solved_modes(inverse, rows)
    new_mode, factor = finish(inverse, upper, sums, fresh, rows, total)
    return (new_modes.reshape(basis.shape), new_mode.reshape(basis.shape[:-1]), factor)


def solution(mesh):
    in_specs = (P(None, "gx", "gy", None), P(None, "gx", "gy", None, None), P())
    out_specs = (P(None, "gx", "gy", None, None), P(None, "gx", "gy", None), P())
    return jax.shard_map(local, mesh=mesh, in_specs=in_specs, out_specs=out_specs, check_vma=False)
```

```python
import jax
import jax.numpy as jnp
from jax import lax
from jax.experimental import pallas as pl
from jax.experimental.pallas import tpu as pltpu
from jax.sharding import PartitionSpec as P

STRIDE = 8
TILE = 128
PIVOTS = 32
F32 = jnp.float32
BF16 = jnp.bfloat16
HIGHEST = lax.Precision.HIGHEST


def swap(block, axis, step):
    return lax.ppermute(block, axis, [(i, i ^ step) for i in range(lax.axis_size(axis))])


def bit_groups(size):
    groups, bit = [], 1
    while bit < size:
        groups.append((bit, 2 * bit, 3 * bit) if 4 * bit <= size else (bit,))
        bit *= 4 if 4 * bit <= size else 2
    return groups


def contract_rows(a, b, precision=None):
    return lax.dot_general(
        a, b, (((0,), (0,)), ((), ())), precision=precision, preferred_element_type=F32
    )


def contract_lanes(a, b, precision=None):
    return lax.dot_general(
        a, b, (((1,), (1,)), ((), ())), precision=precision, preferred_element_type=F32
    )


def packed_blocks(chunks):
    whole = chunks - chunks // 4
    blocks = [(p, c) for p in range(chunks) for c in range(p, chunks) if p < c or p < whole]
    guests = {i: (whole + i // 3, i % 3) for i in range(3 * (chunks // 4))}
    return blocks, guests


def gram_kernel(side_ref, rows_ref, out_ref):
    blocks, guests = packed_blocks(rows_ref.shape[1] // TILE)
    half, edge = out_ref.shape[0], TILE // 2
    lane = lax.broadcasted_iota(jnp.int32, (edge, TILE), 1)
    for side in range(2):

        @pl.when(side_ref[0] == side)
        def _():
            tops = range(half * side, half * (side + 1), edge)
            panels = {}
            for p in sorted({blocks[top // TILE][0] for top in tops}):
                last = max(blocks[top // TILE][1] for top in tops if blocks[top // TILE][0] == p)
                panels[p] = contract_rows(
                    rows_ref[:, TILE * p : TILE * (p + 1)], rows_ref[:, TILE * p : TILE * (last + 1)]
                )
            for top in tops:
                p, c = blocks[top // TILE]
                low = top % TILE
                value = panels[p][low : low + edge, TILE * (c - p) : TILE * (c - p + 1)]
                if p == c and low and p in guests:
                    guest, quarter = guests[p]
                    if guest not in panels:
                        own = rows_ref[:, TILE * guest : TILE * (guest + 1)]
                        panels[guest] = contract_rows(own, own)
                    part = panels[guest][edge:, :TILE] if quarter == 2 else panels[guest][:edge, :TILE]
                    value = jnp.where(lane < edge, pltpu.roll(part, edge, 1) if quarter else part, value)
                out_ref[top - half * side : top - half * side + edge, :] = value


def half_gram(side, rows):
    count, modes = rows.shape
    height = TILE * len(packed_blocks(modes // TILE)[0]) // 2
    return pl.pallas_call(
        gram_kernel,
        out_shape=jax.ShapeDtypeStruct((height, TILE), F32),
        in_specs=[pl.BlockSpec(memory_space=pltpu.SMEM), pl.BlockSpec(memory_space=pltpu.VMEM)],
        cost_estimate=pl.CostEstimate(
            flops=2 * count * height * TILE, bytes_accessed=4 * height * TILE, transcendentals=0
        ),
        compiler_params=pltpu.CompilerParams(vmem_limit_bytes=4 << 20),
        name="gram",
    )(side.reshape(1), rows)


def weights(taps_ref, direction, lag):
    line = taps_ref[...].astype(F32)[direction : direction + 1, :]
    found = jnp.zeros(lag.shape, F32)
    for tap in range(2 * STRIDE + 1):
        value = jnp.broadcast_to(line[:, tap : tap + 1], (1, lag.shape[1]))
        found = jnp.where(lag == tap, value, found)
    return found


def parted(index, size, bound):
    if size & (size - 1) == 0:
        return index >> (size.bit_length() - 1), index & (size - 1)
    scale = -(-(1 << 16) // size)
    assert all((i * scale) >> 16 == i // size for i in range(bound))
    quotient = (index * scale) >> 16
    return quotient, index - size * quotient


def filter_kernel(
    taps_hbm, cells_hbm, out_ref, taps_ref, band, cells, arrived, *, comps, cells_x, cells_y
):
    taps_copy = pltpu.make_async_copy(taps_hbm, taps_ref, arrived.at[0])
    cells_copy = pltpu.make_async_copy(cells_hbm, cells, arrived.at[1])
    taps_copy.start()
    cells_copy.start()
    depth, points = band.shape
    height = out_ref.shape[0]
    z = lax.broadcasted_iota(jnp.int32, (TILE, points), 0)
    p = lax.broadcasted_iota(jnp.int32, (TILE, points), 1)
    lag = z - STRIDE * p + STRIDE
    taps_copy.wait()
    pattern = weights(taps_ref, 2, jnp.where(lag < 0, lag + depth, lag))
    for block in range(depth // TILE):
        turned = pltpu.roll(pattern, TILE // STRIDE * block, 1) if block else pattern
        band[TILE * block : TILE * (block + 1), :] = turned.astype(BF16)
    count = cells.shape[0]
    per_y = cells_y // STRIDE
    out = lax.broadcasted_iota(jnp.int32, (height, count), 0)
    cell = lax.broadcasted_iota(jnp.int32, (height, count), 1)
    slot, within = parted(out, height // 9, height)
    kind, r = parted(slot, 3, 9)
    comp, q = parted(within, per_y, height // 9)
    rest, y = parted(cell, cells_y, count)
    cell_comp, x = parted(rest, cells_x, count)
    y = y + jnp.where(kind == 1, -cells_y, jnp.where(kind == 2, cells_y, 0))
    weight = weights(taps_ref, 0, x - STRIDE * (r - 1) + STRIDE)
    weight = weight * weights(taps_ref, 1, y - STRIDE * q + STRIDE)
    weight = jnp.where(cell_comp == comp, weight, 0.0)
    cells_copy.wait()
    along_z = jnp.dot(cells[...], band[...], preferred_element_type=F32)
    out_ref[...] = jnp.dot(weight, along_z, precision=HIGHEST, preferred_element_type=F32)


def local_filter(taps, snapshot):
    comps, cells_x, cells_y, cells_z = snapshot.shape
    assert cells_x == STRIDE
    points = cells_z // STRIDE
    height = 9 * padded_rows(comps * cells_y // STRIDE)
    cells = snapshot.reshape(-1, cells_z)
    return pl.pallas_call(
        lambda *refs: filter_kernel(*refs, comps=comps, cells_x=cells_x, cells_y=cells_y),
        out_shape=jax.ShapeDtypeStruct((height, points), F32),
        in_specs=[pl.BlockSpec(memory_space=pltpu.HBM)] * 2,
        scratch_shapes=[
            pltpu.VMEM(taps.shape, BF16),
            pltpu.VMEM((cells_z, points), BF16),
            pltpu.VMEM(cells.shape, BF16),
            pltpu.SemaphoreType.DMA((2,)),
        ],
        cost_estimate=pl.CostEstimate(
            flops=4 * cells.size * points, bytes_accessed=2 * cells.size, transcendentals=0
        ),
        compiler_params=pltpu.CompilerParams(vmem_limit_bytes=4 << 20),
        name="filter",
    )(*(pltpu.with_memory_space_constraint(array, pltpu.HBM) for array in (taps, cells)))


def padded_rows(rows):
    return -(-rows // 8) * 8


def along_slabs_y(parts):
    height = parts.shape[0] // 3
    own, up, down = parts[:height], parts[height : 2 * height], parts[2 * height :]
    count = lax.axis_size("gy")
    if count == 2:
        return own + swap(jnp.where(lax.axis_index("gy") == 1, down, up), "gy", 1)
    pairs = [(i, i + 1) for i in range(count - 1)]
    low = lax.ppermute(up, "gy", pairs)
    return own + low + lax.ppermute(down, "gy", [(j, i) for i, j in pairs])


def cross_kernel(own_ref, low_ref, high_ref, rows_ref, fresh_ref, out_ref):
    lines, points = fresh_ref.shape
    modes = rows_ref.shape[1]
    fresh = (own_ref[...] + low_ref[...] + high_ref[...]).astype(BF16).astype(F32)
    fresh_ref[...] = fresh[:lines, :]
    total = jnp.zeros((8, modes), F32)
    square = jnp.zeros((1, 1), F32)
    for i in range(lines):
        line = fresh[i : i + 1, :]
        square = square + jnp.sum(line * line, axis=1, keepdims=True)
        left = jnp.broadcast_to(line, (8, points)).astype(BF16)
        total = total + jnp.dot(
            left, rows_ref[points * i : points * (i + 1), :], preferred_element_type=F32
        )
    out_ref[...] = jnp.zeros(out_ref.shape, F32)
    for c in range(modes // TILE):
        out_ref[c : c + 1, :] = total[:1, TILE * c : TILE * (c + 1)]
    out_ref[modes // TILE : modes // TILE + 1, :] = jnp.broadcast_to(square, (1, TILE))


def local_cross(own, low, high, rows):
    points = own.shape[1]
    return pl.pallas_call(
        cross_kernel,
        out_shape=(
            jax.ShapeDtypeStruct((rows.shape[0] // points, points), F32),
            jax.ShapeDtypeStruct((padded_rows(rows.shape[1] // TILE + 1), TILE), F32),
        ),
        cost_estimate=pl.CostEstimate(flops=16 * rows.size, bytes_accessed=2 * rows.size, transcendentals=0),
        compiler_params=pltpu.CompilerParams(vmem_limit_bytes=4 << 20),
        name="cross",
    )(own, low, high, rows)


def split(value):
    parts = []
    for _ in range(3):
        parts.append(value.astype(BF16))
        value = value - parts[-1].astype(F32)
    return parts


def left_parts(value):
    a, b, c = split(value)
    return jnp.concatenate([a, a, b, b, a, c])


def right_parts(value):
    a, b, c = split(value)
    return jnp.concatenate([a, b, a, b, c, a])


def factor_blocks(work, scaled, upper):
    modes = work.shape[0]
    chunks = modes // TILE
    groups = PIVOTS // 8
    lane = lax.broadcasted_iota(jnp.int32, (8, TILE), 1)
    row = lax.broadcasted_iota(jnp.int32, (8, TILE), 0)
    scale_blocks = []
    for p in range(chunks):
        base = p * TILE
        for j in range(TILE // PIVOTS):
            first = PIVOTS * j
            top = base + first
            rows = [
                [work[top + 8 * g : top + 8 * g + 8, TILE * c : TILE * (c + 1)] for c in range(chunks)]
                for g in range(groups)
            ]
            cols = [
                [
                    jnp.broadcast_to(rows[g][p][:, first + k : first + k + 1], (8, TILE))
                    if g >= k // 8
                    else None
                    for g in range(groups)
                ]
                for k in range(PIVOTS)
            ]
            unit = [jnp.where(lane == first + 8 * g + row, 1.0, 0.0).astype(F32) for g in range(groups)]
            inverse = [jnp.zeros((8, TILE), F32) for _ in range(groups)]
            scale = [jnp.zeros((8, TILE), F32) for _ in range(groups)]
            for k in range(PIVOTS):
                own, sub = k // 8, k % 8
                pivot = cols[k][own][sub : sub + 1, :]
                recip = 1.0 / pivot
                inverse[own] = jnp.where(row == sub, recip, inverse[own])
                scale[own] = jnp.where(row == sub, lax.rsqrt(pivot), scale[own])
                mult = {g: cols[k][g] * recip for g in range(own, groups)}
                for later in range(k + 1, PIVOTS):
                    factor = cols[k][later // 8][later % 8 : later % 8 + 1, :]
                    for g in range(later // 8, groups):
                        cols[later][g] = cols[later][g] - mult[g] * factor
                mult[own] = jnp.where(row > sub, mult[own], 0.0)
                for c in range(chunks):
                    pivot_row = rows[own][c][sub : sub + 1, :]
                    for g in range(own, groups):
                        rows[g][c] = rows[g][c] - mult[g] * pivot_row
                pivot_row = unit[own][sub : sub + 1, :]
                for g in range(own, groups):
                    unit[g] = unit[g] - mult[g] * pivot_row
            inside = (lane >= first) & (lane < first + PIVOTS)
            for g in range(groups):
                where = slice(top + 8 * g, top + 8 * g + 8)
                for c in range(chunks):
                    cut = slice(TILE * c, TILE * (c + 1))
                    if c < p:
                        upper[where, cut] = jnp.zeros((8, TILE), F32)
                    elif c == p:
                        upper[where, cut] = jnp.where(
                            lane >= first + 8 * g + row, rows[g][c] * scale[g], 0.0
                        )
                    else:
                        upper[where, cut] = rows[g][c] * scale[g]
                    if c >= p:
                        scaled[first + 8 * g : first + 8 * g + 8, cut] = rows[g][c] * inverse[g]
                    work[where, cut] = jnp.where(inside, unit[g], rows[g][c]) if c == p else rows[g][c]
                scale_blocks.append(scale[g])
            end = first + PIVOTS
            if end < TILE:
                left = left_parts(jnp.concatenate([rows[g][p] * inverse[g] for g in range(groups)]))
                wide = lax.broadcasted_iota(jnp.int32, (TILE - end, TILE), 1)
                for cuts in ([p], [c for c in range(chunks) if c != p]):
                    right = [work[top : top + PIVOTS, TILE * c : TILE * (c + 1)] for c in cuts]
                    change = contract_rows(left, right_parts(jnp.concatenate(right, axis=1)))
                    for at, c in enumerate(cuts):
                        cut = slice(TILE * c, TILE * (c + 1))
                        old = work[base + end : base + TILE, cut]
                        if c == p:
                            old = jnp.where((wide >= first) & (wide < end), 0.0, old)
                        work[base + end : base + TILE, cut] = old - change[end:, TILE * at : TILE * (at + 1)]
        block_lane = lax.broadcasted_iota(jnp.int32, (TILE, TILE), 1)
        block_row = lax.broadcasted_iota(jnp.int32, (TILE, TILE), 0)
        own = slice(base, base + TILE)
        work[own, own] = jnp.where(block_lane <= block_row, work[own, own], 0.0)
        if p + 1 < chunks:
            left = left_parts(scaled[:, base + TILE :])
            right = right_parts(work[own, :])
        for i in range(p + 1, chunks):
            below = slice(TILE * i, TILE * (i + 1))
            part = left[:, TILE * (i - p - 1) : TILE * (i - p)]
            inverse_part = contract_rows(part, right[:, : base + TILE])
            if p:
                work[below, :base] = work[below, :base] - inverse_part[:, :base]
            work[below, own] = -inverse_part[:, base:]
            gram_part = contract_rows(part, right[:, TILE * i :])
            work[below, TILE * i :] = work[below, TILE * i :] - gram_part
    return scale_blocks


def factor_kernel(side_ref, member_ref, mine_ref, other_ref, inverse_ref, factor_ref, scaled, blocks, *, total):
    work = inverse_ref
    modes = work.shape[0]
    chunks = modes // TILE
    half = blocks.shape[0] // 2
    piece = half // 4
    for part_ref, side in ((mine_ref, side_ref[0]), (other_ref, 1 - side_ref[0])):
        for step in range(4):
            at = pl.multiple_of(half * side + piece * (member_ref[0] ^ step), 8)
            blocks[pl.ds(at, piece), :] = part_ref[piece * step : piece * (step + 1), :] * (1.0 / total)
    places, guests = packed_blocks(chunks)
    for at, (p, c) in enumerate(places):
        work[TILE * p : TILE * (p + 1), TILE * c : TILE * (c + 1)] = blocks[TILE * at : TILE * (at + 1), :]
    edge = TILE // 2
    lane = lax.broadcasted_iota(jnp.int32, (edge, TILE), 1)
    corners = {}
    for p, guest in guests.items():
        at = TILE * places.index((p, p)) + edge
        corners[guest] = blocks[at : at + edge, :]
    for guest in sorted({guest for guest, _ in corners}):
        top, cut = TILE * guest, slice(TILE * guest, TILE * (guest + 1))
        work[top : top + edge, cut] = jnp.where(
            lane < edge, corners[guest, 0], pltpu.roll(corners[guest, 1], edge, 1)
        )
        work[top + edge : top + TILE, cut] = jnp.where(lane < edge, 0.0, pltpu.roll(corners[guest, 2], edge, 1))
    scales = factor_blocks(work, scaled, factor_ref)
    for g, scale in enumerate(scales):
        where = slice(8 * g, 8 * g + 8)
        for c in range(8 * g // TILE + 1):
            work[where, TILE * c : TILE * (c + 1)] = work[where, TILE * c : TILE * (c + 1)] * scale


def factored(side, member, mine, other, modes, total):
    height = TILE * len(packed_blocks(modes // TILE)[0])
    smem, vmem = (pl.BlockSpec(memory_space=space) for space in (pltpu.SMEM, pltpu.VMEM))
    return pl.pallas_call(
        lambda *refs: factor_kernel(*refs, total=total),
        out_shape=(jax.ShapeDtypeStruct((modes, modes), F32),) * 2,
        in_specs=[smem, smem, vmem, vmem],
        scratch_shapes=[pltpu.VMEM((TILE, modes), F32), pltpu.VMEM((height, TILE), F32)],
        cost_estimate=pl.CostEstimate(
            flops=16 * modes**3, bytes_accessed=8 * modes * modes, transcendentals=modes
        ),
        compiler_params=pltpu.CompilerParams(vmem_limit_bytes=10 << 20),
        name="factor",
    )(side.reshape(1), member.reshape(1), mine, other)


def modes_kernel(inverse_ref, rows_ref, modes_ref):
    for p in range(inverse_ref.shape[0] // TILE):
        own = slice(TILE * p, TILE * (p + 1))
        width = TILE * (p + 1)
        known = inverse_ref[own, :width]
        first = known.astype(BF16)
        second = (known - first.astype(F32)).astype(BF16)
        left = rows_ref[:, :width]
        solved = contract_lanes(left, first) + contract_lanes(left, second)
        modes_ref[:, own] = solved.astype(BF16)


def solved_modes(inverse, rows):
    count, modes = rows.shape
    return pl.pallas_call(
        modes_kernel,
        out_shape=jax.ShapeDtypeStruct((count, modes), BF16),
        cost_estimate=pl.CostEstimate(
            flops=4 * count * modes * modes, bytes_accessed=4 * modes * modes, transcendentals=0
        ),
        compiler_params=pltpu.CompilerParams(vmem_limit_bytes=8 << 20),
        name="modes",
    )(inverse, rows)


def finish_kernel(inverse_ref, upper_ref, sums_ref, fresh_ref, rows_ref, mode_ref, factor_ref, *, total):
    modes = inverse_ref.shape[0]
    chunks = modes // TILE
    sums = sums_ref[...] * (1.0 / total)
    cross = [sums[c : c + 1, :] for c in range(chunks)]
    square = sums[chunks : chunks + 1, :]
    projected = []
    for p in range(chunks):
        own = slice(TILE * p, TILE * (p + 1))
        width = TILE * (p + 1)
        known = inverse_ref[own, :width]
        line = jnp.concatenate(cross[: p + 1], axis=1)
        projected.append(contract_lanes(jnp.broadcast_to(line, (8, width)), known, HIGHEST))
        column = sum(known[:, TILE * c : TILE * (c + 1)] * cross[c] for c in range(p + 1))
        factor_ref[own, :modes] = upper_ref[own, :]
        factor_ref[own, modes : modes + 1] = jnp.sum(column, axis=1, keepdims=True)
    norm = sum(jnp.sum(part * part, axis=1, keepdims=True) for part in projected)
    last = jnp.sqrt(square[:, :1] - norm[:1, :])
    back = []
    for c in range(chunks):
        own = slice(TILE * c, TILE * (c + 1))
        part = jnp.zeros((8, TILE), F32)
        for p in range(c, chunks):
            part = part + jnp.dot(
                projected[p],
                inverse_ref[TILE * p : TILE * (p + 1), own],
                precision=HIGHEST,
                preferred_element_type=F32,
            )
        back.append(part)
    share = jnp.concatenate(back, axis=1)
    first = share.astype(BF16)
    second = (share - first.astype(F32)).astype(BF16)
    points = fresh_ref.shape[1]
    for i in range(fresh_ref.shape[0]):
        left = rows_ref[points * i : points * (i + 1), :]
        covered = contract_lanes(first, left) + contract_lanes(second, left)
        mode_ref[:, points * i : points * (i + 1)] = (fresh_ref[i : i + 1, :] - covered[:1, :]) / last
    factor_ref[modes : modes + 1, :modes] = jnp.zeros((1, modes), F32)
    factor_ref[modes : modes + 1, modes : modes + 1] = last


def finish(inverse, upper, sums, fresh, rows, total):
    count, modes = rows.shape
    return pl.pallas_call(
        lambda *refs: finish_kernel(*refs, total=total),
        out_shape=(
            jax.ShapeDtypeStruct((1, count), F32),
            jax.ShapeDtypeStruct((modes + 1, modes + 1), F32),
        ),
        cost_estimate=pl.CostEstimate(
            flops=64 * modes * modes, bytes_accessed=8 * modes * modes, transcendentals=0
        ),
        compiler_params=pltpu.CompilerParams(vmem_limit_bytes=8 << 20),
        name="finish",
    )(inverse, upper, sums, fresh, rows)


def local(snapshot, basis, taps):
    modes = basis.shape[-1]
    rows = basis.reshape(-1, modes)
    total = rows.shape[0] * lax.axis_size("gx") * lax.axis_size("gy")
    side = lax.axis_index("gy") & 1
    place = lax.axis_index("gx")
    member = place & 3
    slabs = lax.axis_size("gx")
    first, *others = bit_groups(slabs)

    parts = local_filter(taps, snapshot)
    side, parts = lax.optimization_barrier((side, parts))
    parts = along_slabs_y(parts)
    away = swap(half_gram(1 - side, rows), "gy", 1)
    half = half_gram(side, rows) + away
    bit = 2
    while bit < lax.axis_size("gy"):
        half = half + swap(half, "gy", bit)
        bit *= 2

    piece = half.shape[0] // 4
    height = parts.shape[0] // 3
    quarters = half.reshape(4, piece, TILE)

    def quarter_of(index):
        return lax.dynamic_index_in_dim(quarters, index, 0, keepdims=False)

    before, own, after = parts[:height], parts[height : 2 * height], parts[2 * height :]
    odd = (member & 1) == 1
    riders = {1: jnp.where(odd, before, after), 3: jnp.where(odd, after, before)}
    got = {}
    for step in first:
        block = quarter_of(member ^ step)
        got[step] = swap(jnp.concatenate([block, riders[step]]) if step in riders else block, "gx", step)
    quarter = sum([got[step][:piece] for step in first], quarter_of(member))
    near, far = got[1][piece:], got[3][piece:]

    if slabs == 16:
        got = {}
        for step in others[0]:
            block = jnp.concatenate([quarter, far]) if step != 8 else quarter
            got[step] = swap(block, "gx", step)
        quarter = sum([block[:piece] for block in got.values()], quarter)
        group = place >> 2
        wanted = jnp.where(member == 0, group - 1, group + 1) & 3
        outer = jnp.where((group ^ wanted) == 1, got[4][piece:], got[12][piece:])
        far = jnp.where((member == 0) | (member == 3), outer, far)
    else:
        for steps in others:
            quarter = sum([swap(quarter, "gx", step) for step in steps], quarter)
        forward = [(i, (i + 1) % slabs) for i in range(slabs)]
        near = lax.ppermute(after, "gx", forward)
        far = lax.ppermute(before, "gx", [(j, i) for i, j in forward])

    fresh, cross = local_cross(own, near, far, rows)
    block = jnp.concatenate([quarter, cross])
    gathered = [block] + [swap(block, "gx", step) for step in first]
    sums = sum([got[piece:] for got in gathered[1:]], block[piece:])
    mine = jnp.concatenate([got[:piece] for got in gathered] + [sums])
    other = swap(mine, "gy", 1)
    sums = mine[4 * piece :] + other[4 * piece :]
    bit = 2
    while bit < lax.axis_size("gy"):
        sums = sums + swap(sums, "gy", bit)
        bit *= 2
    bit = 4
    while 2 * bit < slabs:
        sums = sums + swap(sums, "gx", bit)
        bit *= 2
    inverse, upper = factored(side, member, mine, other, modes, total)
    sums, inverse = lax.optimization_barrier((sums, inverse))
    if bit < slabs:
        sums = sums + swap(sums, "gx", bit)
    new_modes = solved_modes(inverse, rows)
    new_mode, factor = finish(inverse, upper, sums, fresh, rows, total)
    return (new_modes.reshape(basis.shape), new_mode.reshape(basis.shape[:-1]), factor)


def solution(mesh):
    in_specs = (P(None, "gx", "gy", None), P(None, "gx", "gy", None, None), P())
    out_specs = (P(None, "gx", "gy", None, None), P(None, "gx", "gy", None), P())
    return jax.shard_map(local, mesh=mesh, in_specs=in_specs, out_specs=out_specs, check_vma=False)
```

```python
import jax
import jax.numpy as jnp
from jax import lax
from jax.experimental import pallas as pl
from jax.experimental.pallas import tpu as pltpu
from jax.sharding import PartitionSpec as P


STRIDE = 8
TILE = 128
PIVOTS = 32
F32 = jnp.float32
BF16 = jnp.bfloat16
HIGHEST = lax.Precision.HIGHEST


def swap(block, axis, step):
    return lax.ppermute(block, axis, [(i, i ^ step) for i in range(lax.axis_size(axis))])


def swap_by_side(block, steps):
    wide = lax.axis_size("gy")
    pairs = [
        (i * wide + j, (i ^ steps[j & 1]) * wide + j) for i in range(lax.axis_size("gx")) for j in range(wide)
    ]
    return lax.ppermute(block, ("gx", "gy"), pairs)


def bit_groups(size):
    groups, bit = [], 1
    while bit < size:
        groups.append((bit, 2 * bit, 3 * bit) if 4 * bit <= size else (bit,))
        bit *= 4 if 4 * bit <= size else 2
    return groups


def contract_rows(a, b, precision=None):
    return lax.dot_general(
        a, b, (((0,), (0,)), ((), ())), precision=precision, preferred_element_type=F32
    )


def contract_lanes(a, b, precision=None):
    return lax.dot_general(
        a, b, (((1,), (1,)), ((), ())), precision=precision, preferred_element_type=F32
    )


def packed_blocks(chunks):
    whole = chunks - chunks // 4
    blocks = [(p, c) for p in range(chunks) for c in range(p, chunks) if p < c or p < whole]
    guests = {i: (whole + i // 3, i % 3) for i in range(3 * (chunks // 4))}
    return blocks, guests


def gram_kernel(side_ref, rows_ref, out_ref):
    blocks, guests = packed_blocks(rows_ref.shape[1] // TILE)
    half, edge = out_ref.shape[0], TILE // 2
    lane = lax.broadcasted_iota(jnp.int32, (edge, TILE), 1)
    for side in range(2):

        @pl.when(side_ref[0] == side)
        def _():
            tops = range(half * side, half * (side + 1), edge)
            panels = {}
            for p in sorted({blocks[top // TILE][0] for top in tops}):
                last = max(blocks[top // TILE][1] for top in tops if blocks[top // TILE][0] == p)
                panels[p] = contract_rows(
                    rows_ref[:, TILE * p : TILE * (p + 1)], rows_ref[:, TILE * p : TILE * (last + 1)]
                )
            for top in tops:
                p, c = blocks[top // TILE]
                low = top % TILE
                value = panels[p][low : low + edge, TILE * (c - p) : TILE * (c - p + 1)]
                if p == c and low and p in guests:
                    guest, quarter = guests[p]
                    if guest not in panels:
                        own = rows_ref[:, TILE * guest : TILE * (guest + 1)]
                        panels[guest] = contract_rows(own, own)
                    part = panels[guest][edge:, :TILE] if quarter == 2 else panels[guest][:edge, :TILE]
                    value = jnp.where(lane < edge, pltpu.roll(part, edge, 1) if quarter else part, value)
                out_ref[top - half * side : top - half * side + edge, :] = value


def half_gram(side, rows):
    count, modes = rows.shape
    height = TILE * len(packed_blocks(modes // TILE)[0]) // 2
    return pl.pallas_call(
        gram_kernel,
        out_shape=jax.ShapeDtypeStruct((height, TILE), F32),
        in_specs=[pl.BlockSpec(memory_space=pltpu.SMEM), pl.BlockSpec(memory_space=pltpu.VMEM)],
        cost_estimate=pl.CostEstimate(
            flops=2 * count * height * TILE, bytes_accessed=4 * height * TILE, transcendentals=0
        ),
        compiler_params=pltpu.CompilerParams(vmem_limit_bytes=4 << 20),
        name="gram",
    )(side.reshape(1), rows)


def weights(taps_ref, direction, lag):
    line = taps_ref[...].astype(F32)[direction : direction + 1, :]
    found = jnp.zeros(lag.shape, F32)
    for tap in range(2 * STRIDE + 1):
        value = jnp.broadcast_to(line[:, tap : tap + 1], (1, lag.shape[1]))
        found = jnp.where(lag == tap, value, found)
    return found


def parted(index, size, bound):
    if size & (size - 1) == 0:
        return index >> (size.bit_length() - 1), index & (size - 1)
    scale = -(-(1 << 16) // size)
    assert all((i * scale) >> 16 == i // size for i in range(bound))
    quotient = (index * scale) >> 16
    return quotient, index - size * quotient


def filter_kernel(taps_hbm, cells_hbm, out_ref, taps_ref, band, cells, arrived, *, cells_x, cells_y):
    taps_copy = pltpu.make_async_copy(taps_hbm, taps_ref, arrived.at[0])
    cells_copy = pltpu.make_async_copy(cells_hbm, cells, arrived.at[1])
    taps_copy.start()
    cells_copy.start()
    depth, points = band.shape
    height = out_ref.shape[0]
    z = lax.broadcasted_iota(jnp.int32, (TILE, points), 0)
    p = lax.broadcasted_iota(jnp.int32, (TILE, points), 1)
    lag = z - STRIDE * p + STRIDE
    taps_copy.wait()
    pattern = weights(taps_ref, 2, jnp.where(lag < 0, lag + depth, lag))
    for block in range(depth // TILE):
        turned = pltpu.roll(pattern, TILE // STRIDE * block, 1) if block else pattern
        band[TILE * block : TILE * (block + 1), :] = turned.astype(BF16)
    count = cells.shape[0]
    per_y = cells_y // STRIDE
    out = lax.broadcasted_iota(jnp.int32, (height, count), 0)
    cell = lax.broadcasted_iota(jnp.int32, (height, count), 1)
    slot, within = parted(out, height // 9, height)
    kind, r = parted(slot, 3, 9)
    comp, q = parted(within, per_y, height // 9)
    rest, y = parted(cell, cells_y, count)
    cell_comp, x = parted(rest, cells_x, count)
    y = y + jnp.where(kind == 1, -cells_y, jnp.where(kind == 2, cells_y, 0))
    weight = weights(taps_ref, 0, x - STRIDE * (r - 1) + STRIDE)
    weight = weight * weights(taps_ref, 1, y - STRIDE * q + STRIDE)
    weight = jnp.where(cell_comp == comp, weight, 0.0)
    cells_copy.wait()
    along_z = jnp.dot(cells[...], band[...], preferred_element_type=F32)
    out_ref[...] = jnp.dot(weight, along_z, precision=HIGHEST, preferred_element_type=F32)


def local_filter(taps, snapshot):
    comps, cells_x, cells_y, cells_z = snapshot.shape
    assert cells_x == STRIDE
    points = cells_z // STRIDE
    height = 9 * padded_rows(comps * cells_y // STRIDE)
    cells = snapshot.reshape(-1, cells_z)
    return pl.pallas_call(
        lambda *refs: filter_kernel(*refs, cells_x=cells_x, cells_y=cells_y),
        out_shape=jax.ShapeDtypeStruct((height, points), F32),
        in_specs=[pl.BlockSpec(memory_space=pltpu.HBM)] * 2,
        scratch_shapes=[
            pltpu.VMEM(taps.shape, BF16),
            pltpu.VMEM((cells_z, points), BF16),
            pltpu.VMEM(cells.shape, BF16),
            pltpu.SemaphoreType.DMA((2,)),
        ],
        cost_estimate=pl.CostEstimate(
            flops=4 * cells.size * points, bytes_accessed=2 * cells.size, transcendentals=0
        ),
        compiler_params=pltpu.CompilerParams(vmem_limit_bytes=4 << 20),
        name="filter",
    )(*(pltpu.with_memory_space_constraint(array, pltpu.HBM) for array in (taps, cells)))


def padded_rows(rows):
    return -(-rows // 8) * 8


def along_slabs_y(parts):
    height = parts.shape[0] // 3
    own, up, down = parts[:height], parts[height : 2 * height], parts[2 * height :]
    count = lax.axis_size("gy")
    if count == 2:
        return own + swap(jnp.where(lax.axis_index("gy") == 1, down, up), "gy", 1)
    pairs = [(i, i + 1) for i in range(count - 1)]
    low = lax.ppermute(up, "gy", pairs)
    return own + low + lax.ppermute(down, "gy", [(j, i) for i, j in pairs])


def cross_kernel(own_ref, low_ref, high_ref, rows_ref, fresh_ref, out_ref):
    lines, points = fresh_ref.shape
    modes = rows_ref.shape[1]
    fresh = (own_ref[...] + low_ref[...] + high_ref[...]).astype(BF16).astype(F32)
    fresh_ref[...] = fresh[:lines, :]
    total = jnp.zeros((8, modes), F32)
    square = jnp.zeros((1, 1), F32)
    for i in range(lines):
        line = fresh[i : i + 1, :]
        square = square + jnp.sum(line * line, axis=1, keepdims=True)
        left = jnp.broadcast_to(line, (8, points)).astype(BF16)
        total = total + jnp.dot(
            left, rows_ref[points * i : points * (i + 1), :], preferred_element_type=F32
        )
    out_ref[...] = jnp.zeros(out_ref.shape, F32)
    for c in range(modes // TILE):
        out_ref[c : c + 1, :] = total[:1, TILE * c : TILE * (c + 1)]
    out_ref[modes // TILE : modes // TILE + 1, :] = jnp.broadcast_to(square, (1, TILE))


def local_cross(own, low, high, rows):
    points = own.shape[1]
    return pl.pallas_call(
        cross_kernel,
        out_shape=(
            jax.ShapeDtypeStruct((rows.shape[0] // points, points), F32),
            jax.ShapeDtypeStruct((padded_rows(rows.shape[1] // TILE + 1), TILE), F32),
        ),
        cost_estimate=pl.CostEstimate(flops=16 * rows.size, bytes_accessed=2 * rows.size, transcendentals=0),
        compiler_params=pltpu.CompilerParams(vmem_limit_bytes=4 << 20),
        name="cross",
    )(own, low, high, rows)


def split(value):
    parts = []
    for _ in range(3):
        parts.append(value.astype(BF16))
        value = value - parts[-1].astype(F32)
    return parts


def left_parts(value):
    a, b, c = split(value)
    return jnp.concatenate([a, a, b, b, a, c])


def right_parts(value):
    a, b, c = split(value)
    return jnp.concatenate([a, b, a, b, c, a])


def factor_blocks(work, scaled, upper, panels, after):
    modes = work.shape[0]
    chunks = modes // TILE
    groups = PIVOTS // 8
    lane = lax.broadcasted_iota(jnp.int32, (8, TILE), 1)
    row = lax.broadcasted_iota(jnp.int32, (8, TILE), 0)
    for p in panels:
        base = p * TILE
        shift = panels[0] * TILE
        scale_blocks = []
        for j in range(TILE // PIVOTS):
            first = PIVOTS * j
            top = base + first
            rows = [
                [work[top + 8 * g : top + 8 * g + 8, TILE * c : TILE * (c + 1)] for c in range(chunks)]
                for g in range(groups)
            ]
            cols = [
                [
                    jnp.broadcast_to(rows[g][p][:, first + k : first + k + 1], (8, TILE))
                    if g >= k // 8
                    else None
                    for g in range(groups)
                ]
                for k in range(PIVOTS)
            ]
            unit = [jnp.where(lane == first + 8 * g + row, 1.0, 0.0).astype(F32) for g in range(groups)]
            inverse = [jnp.zeros((8, TILE), F32) for _ in range(groups)]
            scale = [jnp.zeros((8, TILE), F32) for _ in range(groups)]
            for k in range(PIVOTS):
                own, sub = k // 8, k % 8
                pivot = cols[k][own][sub : sub + 1, :]
                recip = 1.0 / pivot
                inverse[own] = jnp.where(row == sub, recip, inverse[own])
                scale[own] = jnp.where(row == sub, lax.rsqrt(pivot), scale[own])
                mult = {g: cols[k][g] * recip for g in range(own, groups)}
                for later in range(k + 1, PIVOTS):
                    factor = cols[k][later // 8][later % 8 : later % 8 + 1, :]
                    for g in range(later // 8, groups):
                        cols[later][g] = cols[later][g] - mult[g] * factor
                mult[own] = jnp.where(row > sub, mult[own], 0.0)
                for c in range(chunks):
                    pivot_row = rows[own][c][sub : sub + 1, :]
                    for g in range(own, groups):
                        rows[g][c] = rows[g][c] - mult[g] * pivot_row
                pivot_row = unit[own][sub : sub + 1, :]
                for g in range(own, groups):
                    unit[g] = unit[g] - mult[g] * pivot_row
            inside = (lane >= first) & (lane < first + PIVOTS)
            for g in range(groups):
                where = slice(top + 8 * g, top + 8 * g + 8)
                line = slice(top - shift + 8 * g, top - shift + 8 * g + 8)
                for c in range(chunks):
                    cut = slice(TILE * c, TILE * (c + 1))
                    if c < p:
                        upper[line, cut] = jnp.zeros((8, TILE), F32)
                    elif c == p:
                        upper[line, cut] = jnp.where(
                            lane >= first + 8 * g + row, rows[g][c] * scale[g], 0.0
                        )
                    else:
                        upper[line, cut] = rows[g][c] * scale[g]
                    if c >= p:
                        scaled[first + 8 * g : first + 8 * g + 8, cut] = rows[g][c] * inverse[g]
                    work[where, cut] = jnp.where(inside, unit[g], rows[g][c]) if c == p else rows[g][c]
                scale_blocks.append(scale[g])
            end = first + PIVOTS
            if end < TILE:
                left = left_parts(jnp.concatenate([rows[g][p] * inverse[g] for g in range(groups)]))
                wide = lax.broadcasted_iota(jnp.int32, (TILE - end, TILE), 1)
                for cuts in ([p], [c for c in range(chunks) if c != p]):
                    right = [work[top : top + PIVOTS, TILE * c : TILE * (c + 1)] for c in cuts]
                    change = contract_rows(left, right_parts(jnp.concatenate(right, axis=1)))
                    for at, c in enumerate(cuts):
                        cut = slice(TILE * c, TILE * (c + 1))
                        old = work[base + end : base + TILE, cut]
                        if c == p:
                            old = jnp.where((wide >= first) & (wide < end), 0.0, old)
                        work[base + end : base + TILE, cut] = old - change[end:, TILE * at : TILE * (at + 1)]
        block_lane = lax.broadcasted_iota(jnp.int32, (TILE, TILE), 1)
        block_row = lax.broadcasted_iota(jnp.int32, (TILE, TILE), 0)
        own = slice(base, base + TILE)
        work[own, own] = jnp.where(block_lane <= block_row, work[own, own], 0.0)
        if p + 1 < chunks:
            left = left_parts(scaled[:, base + TILE :])
            right = right_parts(work[own, :])
        for i in range(p + 1, chunks):
            below = slice(TILE * i, TILE * (i + 1))
            part = left[:, TILE * (i - p - 1) : TILE * (i - p)]
            inverse_part = contract_rows(part, right[:, : base + TILE])
            if p:
                work[below, :base] = work[below, :base] - inverse_part[:, :base]
            work[below, own] = -inverse_part[:, base:]
            gram_part = contract_rows(part, right[:, TILE * i :])
            work[below, TILE * i :] = work[below, TILE * i :] - gram_part
        for g, scale in enumerate(scale_blocks):
            where = slice(base + 8 * g, base + 8 * g + 8)
            for c in range(p + 1):
                cut = slice(TILE * c, TILE * (c + 1))
                work[where, cut] = work[where, cut] * scale
        after(p)


def early_kernel(side_ref, member_ref, beside_ref, mine_ref, other_ref, work, upper, scaled, blocks, *, total):
    modes = work.shape[0]
    chunks = modes // TILE
    half = blocks.shape[0] // 2
    piece = half // 4
    sides = ((mine_ref, side_ref[0], member_ref[0]), (other_ref, 1 - side_ref[0], beside_ref[0]))
    for part_ref, side, member in sides:
        for step in range(4):
            at = pl.multiple_of(half * side + piece * (member ^ step), 8)
            blocks[pl.ds(at, piece), :] = part_ref[piece * step : piece * (step + 1), :] * (1.0 / total)
    places, guests = packed_blocks(chunks)
    for at, (p, c) in enumerate(places):
        work[TILE * p : TILE * (p + 1), TILE * c : TILE * (c + 1)] = blocks[TILE * at : TILE * (at + 1), :]
    edge = TILE // 2
    lane = lax.broadcasted_iota(jnp.int32, (edge, TILE), 1)
    corners = {}
    for p, guest in guests.items():
        at = TILE * places.index((p, p)) + edge
        corners[guest] = blocks[at : at + edge, :]
    for guest in sorted({guest for guest, _ in corners}):
        top, cut = TILE * guest, slice(TILE * guest, TILE * (guest + 1))
        work[top : top + edge, cut] = jnp.where(
            lane < edge, corners[guest, 0], pltpu.roll(corners[guest, 1], edge, 1)
        )
        work[top + edge : top + TILE, cut] = jnp.where(lane < edge, 0.0, pltpu.roll(corners[guest, 2], edge, 1))
    factor_blocks(work, scaled, upper, range(chunks // 2), lambda p: None)


def early_panels(side, member, beside, mine, other, modes, total):
    height = TILE * len(packed_blocks(modes // TILE)[0])
    smem, vmem = (pl.BlockSpec(memory_space=space) for space in (pltpu.SMEM, pltpu.VMEM))
    return pl.pallas_call(
        lambda *refs: early_kernel(*refs, total=total),
        out_shape=(
            jax.ShapeDtypeStruct((modes, modes), F32),
            jax.ShapeDtypeStruct((modes // TILE // 2 * TILE, modes), F32),
        ),
        in_specs=[smem, smem, smem, vmem, vmem],
        scratch_shapes=[pltpu.VMEM((TILE, modes), F32), pltpu.VMEM((height, TILE), F32)],
        cost_estimate=pl.CostEstimate(
            flops=16 * modes**3, bytes_accessed=8 * modes * modes, transcendentals=modes
        ),
        compiler_params=pltpu.CompilerParams(vmem_limit_bytes=8 << 20),
        name="early",
    )(side.reshape(1), member.reshape(1), beside.reshape(1), mine, other)


def late_kernel(
    early_ref, early_upper_ref, rows_ref, inverse_ref, modes_hbm, factor_hbm, scaled, upper, solved, sent
):
    modes = inverse_ref.shape[0]
    chunks = modes // TILE
    above = early_upper_ref.shape[0]
    copies = [pltpu.make_async_copy(early_upper_ref, factor_hbm.at[:above, :modes], sent.at[chunks])]
    copies[0].start()
    inverse_ref[...] = early_ref[...]

    def solve(p):
        own = slice(TILE * p, TILE * (p + 1))
        width = TILE * (p + 1)
        known = inverse_ref[own, :width]
        first = known.astype(BF16)
        second = (known - first.astype(F32)).astype(BF16)
        left = rows_ref[:, :width]
        solved[p] = (contract_lanes(left, first) + contract_lanes(left, second)).astype(BF16)
        copy = pltpu.make_async_copy(solved.at[p], modes_hbm.at[:, own], sent.at[p])
        copy.start()
        copies.append(copy)

    for p in range(chunks // 2):
        solve(p)
    factor_blocks(inverse_ref, scaled, upper, range(chunks // 2, chunks), solve)
    upper[modes - above : modes - above + 1, :] = jnp.zeros((1, modes), F32)
    copy = pltpu.make_async_copy(upper, factor_hbm.at[above:, :modes], sent.at[chunks + 1])
    copy.start()
    for copy in copies + [copy]:
        copy.wait()


def late_panels(early, early_upper, rows):
    count, modes = rows.shape
    chunks = modes // TILE
    vmem, hbm = (pl.BlockSpec(memory_space=space) for space in (pltpu.VMEM, pltpu.HBM))
    return pl.pallas_call(
        late_kernel,
        out_shape=(
            jax.ShapeDtypeStruct((modes, modes), F32),
            jax.ShapeDtypeStruct((count, modes), BF16),
            jax.ShapeDtypeStruct((modes + 1, modes + 1), F32),
        ),
        out_specs=(vmem, hbm, hbm),
        scratch_shapes=[
            pltpu.VMEM((TILE, modes), F32),
            pltpu.VMEM((modes + 1 - early_upper.shape[0], modes), F32),
            pltpu.VMEM((chunks, count, TILE), BF16),
            pltpu.SemaphoreType.DMA((chunks + 2,)),
        ],
        cost_estimate=pl.CostEstimate(
            flops=16 * modes**3, bytes_accessed=8 * modes * modes, transcendentals=modes
        ),
        compiler_params=pltpu.CompilerParams(vmem_limit_bytes=10 << 20),
        name="late",
    )(early, early_upper, rows)


def finish_kernel(inverse_ref, sums_ref, fresh_ref, rows_ref, _, mode_ref, column_ref, *, total):
    modes = inverse_ref.shape[0]
    chunks = modes // TILE
    sums = sums_ref[...] * (1.0 / total)
    cross = [sums[c : c + 1, :] for c in range(chunks)]
    square = sums[chunks : chunks + 1, :]
    norm = jnp.zeros((1, TILE), F32)
    back = [jnp.zeros((1, TILE), F32)] * chunks
    for p in range(chunks):
        own = slice(TILE * p, TILE * (p + 1))
        known = [inverse_ref[own, TILE * c : TILE * (c + 1)] for c in range(p + 1)]
        column = sum(known[c] * cross[c] for c in range(p + 1))
        column = jnp.broadcast_to(jnp.sum(column, axis=1, keepdims=True), (TILE, TILE))
        column_ref[own, :] = column
        norm = norm + jnp.sum(column * column, axis=0, keepdims=True)
        for c in range(p + 1):
            back[c] = back[c] + jnp.sum(known[c] * column, axis=0, keepdims=True)
    last = jnp.sqrt(square - norm)
    share = jnp.concatenate(back, axis=1)
    first = share.astype(BF16)
    second = (share - first.astype(F32)).astype(BF16)
    both = jnp.concatenate([jnp.broadcast_to(part, (16, modes)) for part in (first, second)])
    points = fresh_ref.shape[1]
    for i in range(fresh_ref.shape[0]):
        left = rows_ref[points * i : points * (i + 1), :]
        covered = contract_lanes(both, left)
        covered = covered[:1, :] + covered[16:17, :]
        mode_ref[:, points * i : points * (i + 1)] = (fresh_ref[i : i + 1, :] - covered) / last
    column_ref[modes : modes + 1, :] = last


def finish(inverse, sums, fresh, rows, factor, total):
    count, modes = rows.shape
    vmem, hbm = (pl.BlockSpec(memory_space=space) for space in (pltpu.VMEM, pltpu.HBM))
    return pl.pallas_call(
        lambda *refs: finish_kernel(*refs, total=total),
        grid=(1,),
        out_shape=(
            jax.ShapeDtypeStruct((1, count), F32),
            jax.ShapeDtypeStruct((modes + 1, modes + 1), F32),
        ),
        in_specs=[vmem, vmem, vmem, vmem, hbm],
        out_specs=(
            pl.BlockSpec((1, count), lambda i: (0, 0)),
            pl.BlockSpec((modes + 1, TILE), lambda i: (0, modes // TILE)),
        ),
        input_output_aliases={4: 1},
        cost_estimate=pl.CostEstimate(
            flops=64 * modes * modes, bytes_accessed=4 * modes * modes, transcendentals=0
        ),
        compiler_params=pltpu.CompilerParams(vmem_limit_bytes=8 << 20),
        name="finish",
    )(inverse, sums, fresh, rows, factor)


def local(snapshot, basis, taps):
    modes = basis.shape[-1]
    rows = basis.reshape(-1, modes)
    total = rows.shape[0] * lax.axis_size("gx") * lax.axis_size("gy")
    side = lax.axis_index("gy") & 1
    place = lax.axis_index("gx")
    inner, group = place & 3, (place >> 2) & 3
    slabs = lax.axis_size("gx")
    near_steps, far_steps, *others = bit_groups(slabs)
    even = side == 0
    member, beside = jnp.where(even, inner, group), jnp.where(even, group, inner)
    ways = (tuple(zip(near_steps, far_steps)), tuple(zip(far_steps, near_steps)))

    parts = local_filter(taps, snapshot)
    side, parts = lax.optimization_barrier((side, parts))
    parts = along_slabs_y(parts)
    away = swap(half_gram(1 - side, rows), "gy", 1)
    half = half_gram(side, rows) + away
    bit = 2
    while bit < lax.axis_size("gy"):
        half = half + swap(half, "gy", bit)
        bit *= 2

    piece = half.shape[0] // 4
    height = parts.shape[0] // 3
    quarters = half.reshape(4, piece, TILE)

    def quarter_of(index):
        return lax.dynamic_index_in_dim(quarters, index, 0, keepdims=False)

    before, own, after = parts[:height], parts[height : 2 * height], parts[2 * height :]
    odd = (inner & 1) == 1
    outer = (inner == 0) | (inner == 3)
    by_one, by_three = jnp.where(odd, before, after), jnp.where(odd, after, before)
    over = jnp.where(inner == 0, before, after)
    wanted = jnp.where((inner == 0) == even, group - 1, group + 1) & 3
    next_group = (group ^ wanted) == 1

    def exchanged(blocks, riders, way):
        return [
            swap_by_side(block if rider is None else jnp.concatenate([block, rider]), steps)
            for block, rider, steps in zip(blocks, riders, way)
        ]

    got = exchanged(
        [quarter_of(member ^ step) for step in (1, 2, 3)],
        (jnp.where(even, by_one, over), None, jnp.where(even, by_three, over)),
        ways[0],
    )
    quarter = sum([block[:piece] for block in got], quarter_of(member))
    one, three = got[0][piece:], got[2][piece:]

    crossed = jnp.where(outer, jnp.where(next_group, one, three), by_three)
    riders = (jnp.where(even, three, by_one), None, jnp.where(even, three, crossed))
    got = exchanged([quarter] * 3, riders, ways[1])
    quarter = sum([block[:piece] for block in got], quarter)
    if slabs == 16:
        last_one, last_three = got[0][piece:], got[2][piece:]
        near = jnp.where(even, one, last_one)
        passed = jnp.where(outer, jnp.where(next_group, last_one, last_three), three)
        far = jnp.where(even, passed, last_three)
    else:
        for steps in others:
            quarter = sum([swap(quarter, "gx", step) for step in steps], quarter)
        forward = [(i, (i + 1) % slabs) for i in range(slabs)]
        near = lax.ppermute(after, "gx", forward)
        far = lax.ppermute(before, "gx", [(j, i) for i, j in forward])

    fresh, cross = local_cross(own, near, far, rows)
    block = jnp.concatenate([quarter, cross])
    gathered = [block] + exchanged([block] * 3, (None,) * 3, ways[0])
    sums = sum([got[piece:] for got in gathered[1:]], block[piece:])
    mine = jnp.concatenate([got[:piece] for got in gathered])
    other = swap(mine, "gy", 1)
    sums = sums + swap_by_side(sums, ways[1][0])
    for steps in others:
        sums = sum([swap(sums, "gx", step) for step in steps], sums)
    bit = 2
    while bit < lax.axis_size("gy"):
        sums = sums + swap(sums, "gy", bit)
        bit *= 2
    hopped = swap_by_side(sums, ways[1][1])
    sums = sums + hopped
    early, early_upper = early_panels(side, member, beside, mine, other, modes, total)
    sums, early = lax.optimization_barrier((sums, early))
    sums = sums + swap(sums, "gy", 1)
    inverse, new_modes, factor = late_panels(early, early_upper, rows)
    new_mode, factor = finish(inverse, sums, fresh, rows, factor, total)
    return (new_modes.reshape(basis.shape), new_mode.reshape(basis.shape[:-1]), factor)


def solution(mesh):
    in_specs = (P(None, "gx", "gy", None), P(None, "gx", "gy", None, None), P())
    out_specs = (P(None, "gx", "gy", None, None), P(None, "gx", "gy", None), P())

    return jax.shard_map(local, mesh=mesh, in_specs=in_specs, out_specs=out_specs, check_vma=False)
```

```python
import jax
import jax.numpy as jnp
from jax import lax
from jax.experimental import pallas as pl
from jax.experimental.pallas import tpu as pltpu
from jax.sharding import PartitionSpec as P


STRIDE = 8
TILE = 128
PIVOTS = 32
F32 = jnp.float32
BF16 = jnp.bfloat16
HIGHEST = lax.Precision.HIGHEST


def swap(block, axis, step):
    return lax.ppermute(block, axis, [(i, i ^ step) for i in range(lax.axis_size(axis))])


def swap_by_side(block, steps):
    wide = lax.axis_size("gy")
    pairs = [
        (i * wide + j, (i ^ steps[j & 1]) * wide + j) for i in range(lax.axis_size("gx")) for j in range(wide)
    ]
    return lax.ppermute(block, ("gx", "gy"), pairs)


def bit_groups(size):
    groups, bit = [], 1
    while bit < size:
        groups.append((bit, 2 * bit, 3 * bit) if 4 * bit <= size else (bit,))
        bit *= 4 if 4 * bit <= size else 2
    return groups


def contract_rows(a, b, precision=None):
    return lax.dot_general(
        a, b, (((0,), (0,)), ((), ())), precision=precision, preferred_element_type=F32
    )


def contract_lanes(a, b, precision=None):
    return lax.dot_general(
        a, b, (((1,), (1,)), ((), ())), precision=precision, preferred_element_type=F32
    )


def packed_blocks(chunks):
    whole = chunks - chunks // 4
    blocks = [(p, c) for p in range(chunks) for c in range(p, chunks) if p < c or p < whole]
    guests = {i: (whole + i // 3, i % 3) for i in range(3 * (chunks // 4))}
    return blocks, guests


def gram_kernel(side_ref, rows_ref, out_ref):
    blocks, guests = packed_blocks(rows_ref.shape[1] // TILE)
    half, edge = out_ref.shape[0], TILE // 2
    lane = lax.broadcasted_iota(jnp.int32, (edge, TILE), 1)
    for side in range(2):

        @pl.when(side_ref[0] == side)
        def _():
            tops = range(half * side, half * (side + 1), edge)
            panels = {}
            for p in sorted({blocks[top // TILE][0] for top in tops}):
                last = max(blocks[top // TILE][1] for top in tops if blocks[top // TILE][0] == p)
                panels[p] = contract_rows(
                    rows_ref[:, TILE * p : TILE * (p + 1)], rows_ref[:, TILE * p : TILE * (last + 1)]
                )
            for top in tops:
                p, c = blocks[top // TILE]
                low = top % TILE
                value = panels[p][low : low + edge, TILE * (c - p) : TILE * (c - p + 1)]
                if p == c and low and p in guests:
                    guest, quarter = guests[p]
                    if guest not in panels:
                        own = rows_ref[:, TILE * guest : TILE * (guest + 1)]
                        panels[guest] = contract_rows(own, own)
                    part = panels[guest][edge:, :TILE] if quarter == 2 else panels[guest][:edge, :TILE]
                    value = jnp.where(lane < edge, pltpu.roll(part, edge, 1) if quarter else part, value)
                out_ref[top - half * side : top - half * side + edge, :] = value


def half_gram(side, rows):
    count, modes = rows.shape
    height = TILE * len(packed_blocks(modes // TILE)[0]) // 2
    return pl.pallas_call(
        gram_kernel,
        out_shape=jax.ShapeDtypeStruct((height, TILE), F32),
        in_specs=[pl.BlockSpec(memory_space=pltpu.SMEM), pl.BlockSpec(memory_space=pltpu.VMEM)],
        cost_estimate=pl.CostEstimate(
            flops=2 * count * height * TILE, bytes_accessed=4 * height * TILE, transcendentals=0
        ),
        compiler_params=pltpu.CompilerParams(vmem_limit_bytes=4 << 20),
        name="gram",
    )(side.reshape(1), rows)


def weights(taps_ref, direction, lag):
    line = taps_ref[...].astype(F32)[direction : direction + 1, :]
    found = jnp.zeros(lag.shape, F32)
    for tap in range(2 * STRIDE + 1):
        value = jnp.broadcast_to(line[:, tap : tap + 1], (1, lag.shape[1]))
        found = jnp.where(lag == tap, value, found)
    return found


def parted(index, size, bound):
    if size & (size - 1) == 0:
        return index >> (size.bit_length() - 1), index & (size - 1)
    scale = -(-(1 << 16) // size)
    assert all((i * scale) >> 16 == i // size for i in range(bound))
    quotient = (index * scale) >> 16
    return quotient, index - size * quotient


def filter_kernel(taps_hbm, cells_hbm, out_ref, taps_ref, band, cells, arrived, *, cells_x, cells_y):
    taps_copy = pltpu.make_async_copy(taps_hbm, taps_ref, arrived.at[0])
    cells_copy = pltpu.make_async_copy(cells_hbm, cells, arrived.at[1])
    taps_copy.start()
    cells_copy.start()
    depth, points = band.shape
    height = out_ref.shape[0]
    z = lax.broadcasted_iota(jnp.int32, (TILE, points), 0)
    p = lax.broadcasted_iota(jnp.int32, (TILE, points), 1)
    lag = z - STRIDE * p + STRIDE
    taps_copy.wait()
    pattern = weights(taps_ref, 2, jnp.where(lag < 0, lag + depth, lag))
    for block in range(depth // TILE):
        turned = pltpu.roll(pattern, TILE // STRIDE * block, 1) if block else pattern
        band[TILE * block : TILE * (block + 1), :] = turned.astype(BF16)
    count = cells.shape[0]
    per_y = cells_y // STRIDE
    out = lax.broadcasted_iota(jnp.int32, (height, count), 0)
    cell = lax.broadcasted_iota(jnp.int32, (height, count), 1)
    slot, within = parted(out, height // 9, height)
    kind, r = parted(slot, 3, 9)
    comp, q = parted(within, per_y, height // 9)
    rest, y = parted(cell, cells_y, count)
    cell_comp, x = parted(rest, cells_x, count)
    y = y + jnp.where(kind == 1, -cells_y, jnp.where(kind == 2, cells_y, 0))
    weight = weights(taps_ref, 0, x - STRIDE * (r - 1) + STRIDE)
    weight = weight * weights(taps_ref, 1, y - STRIDE * q + STRIDE)
    weight = jnp.where(cell_comp == comp, weight, 0.0)
    cells_copy.wait()
    along_z = jnp.dot(cells[...], band[...], preferred_element_type=F32)
    out_ref[...] = jnp.dot(weight, along_z, precision=HIGHEST, preferred_element_type=F32)


def local_filter(taps, snapshot):
    comps, cells_x, cells_y, cells_z = snapshot.shape
    assert cells_x == STRIDE
    points = cells_z // STRIDE
    height = 9 * padded_rows(comps * cells_y // STRIDE)
    cells = snapshot.reshape(-1, cells_z)
    return pl.pallas_call(
        lambda *refs: filter_kernel(*refs, cells_x=cells_x, cells_y=cells_y),
        out_shape=jax.ShapeDtypeStruct((height, points), F32),
        in_specs=[pl.BlockSpec(memory_space=pltpu.HBM)] * 2,
        scratch_shapes=[
            pltpu.VMEM(taps.shape, BF16),
            pltpu.VMEM((cells_z, points), BF16),
            pltpu.VMEM(cells.shape, BF16),
            pltpu.SemaphoreType.DMA((2,)),
        ],
        cost_estimate=pl.CostEstimate(
            flops=4 * cells.size * points, bytes_accessed=2 * cells.size, transcendentals=0
        ),
        compiler_params=pltpu.CompilerParams(vmem_limit_bytes=4 << 20),
        name="filter",
    )(*(pltpu.with_memory_space_constraint(array, pltpu.HBM) for array in (taps, cells)))


def padded_rows(rows):
    return -(-rows // 8) * 8


def along_slabs_y(parts):
    height = parts.shape[0] // 3
    own, up, down = parts[:height], parts[height : 2 * height], parts[2 * height :]
    count = lax.axis_size("gy")
    if count == 2:
        return own + swap(jnp.where(lax.axis_index("gy") == 1, down, up), "gy", 1)
    pairs = [(i, i + 1) for i in range(count - 1)]
    low = lax.ppermute(up, "gy", pairs)
    return own + low + lax.ppermute(down, "gy", [(j, i) for i, j in pairs])


def cross_kernel(own_ref, low_ref, high_ref, rows_ref, fresh_ref, out_ref):
    lines, points = fresh_ref.shape
    modes = rows_ref.shape[1]
    fresh = (own_ref[...] + low_ref[...] + high_ref[...]).astype(BF16).astype(F32)
    fresh_ref[...] = fresh[:lines, :]
    total = jnp.zeros((8, modes), F32)
    square = jnp.zeros((1, 1), F32)
    for i in range(lines):
        line = fresh[i : i + 1, :]
        square = square + jnp.sum(line * line, axis=1, keepdims=True)
        left = jnp.broadcast_to(line, (8, points)).astype(BF16)
        total = total + jnp.dot(
            left, rows_ref[points * i : points * (i + 1), :], preferred_element_type=F32
        )
    out_ref[...] = jnp.zeros(out_ref.shape, F32)
    for c in range(modes // TILE):
        out_ref[c : c + 1, :] = total[:1, TILE * c : TILE * (c + 1)]
    out_ref[modes // TILE : modes // TILE + 1, :] = jnp.broadcast_to(square, (1, TILE))


def local_cross(own, low, high, rows):
    points = own.shape[1]
    return pl.pallas_call(
        cross_kernel,
        out_shape=(
            jax.ShapeDtypeStruct((rows.shape[0] // points, points), F32),
            jax.ShapeDtypeStruct((padded_rows(rows.shape[1] // TILE + 1), TILE), F32),
        ),
        cost_estimate=pl.CostEstimate(flops=16 * rows.size, bytes_accessed=2 * rows.size, transcendentals=0),
        compiler_params=pltpu.CompilerParams(vmem_limit_bytes=4 << 20),
        name="cross",
    )(own, low, high, rows)


def split(value):
    parts = []
    for _ in range(3):
        parts.append(value.astype(BF16))
        value = value - parts[-1].astype(F32)
    return parts


def left_parts(value):
    a, b, c = split(value)
    return jnp.concatenate([a, a, b, b, a, c])


def right_parts(value):
    a, b, c = split(value)
    return jnp.concatenate([a, b, a, b, c, a])


def factor_blocks(work, scaled, upper, panels, after):
    modes = work.shape[0]
    chunks = modes // TILE
    groups = PIVOTS // 8
    lane = lax.broadcasted_iota(jnp.int32, (8, TILE), 1)
    row = lax.broadcasted_iota(jnp.int32, (8, TILE), 0)
    for p in panels:
        base = p * TILE
        shift = panels[0] * TILE
        scale_blocks = []
        for j in range(TILE // PIVOTS):
            first = PIVOTS * j
            top = base + first
            rows = [
                [work[top + 8 * g : top + 8 * g + 8, TILE * c : TILE * (c + 1)] for c in range(chunks)]
                for g in range(groups)
            ]
            cols = [
                [
                    jnp.broadcast_to(rows[g][p][:, first + k : first + k + 1], (8, TILE))
                    if g >= k // 8
                    else None
                    for g in range(groups)
                ]
                for k in range(PIVOTS)
            ]
            unit = [jnp.where(lane == first + 8 * g + row, 1.0, 0.0).astype(F32) for g in range(groups)]
            inverse = [jnp.zeros((8, TILE), F32) for _ in range(groups)]
            for k in range(PIVOTS):
                own, sub = k // 8, k % 8
                pivot = cols[k][own][sub : sub + 1, :]
                recip = 1.0 / pivot
                inverse[own] = jnp.where(row == sub, recip, inverse[own])
                mult = {g: cols[k][g] * recip for g in range(own, groups)}
                for later in range(k + 1, PIVOTS):
                    factor = cols[k][later // 8][later % 8 : later % 8 + 1, :]
                    for g in range(later // 8, groups):
                        cols[later][g] = cols[later][g] - mult[g] * factor
                mult[own] = jnp.where(row > sub, mult[own], 0.0)
                for c in range(chunks):
                    pivot_row = rows[own][c][sub : sub + 1, :]
                    for g in range(own, groups):
                        rows[g][c] = rows[g][c] - mult[g] * pivot_row
                pivot_row = unit[own][sub : sub + 1, :]
                for g in range(own, groups):
                    unit[g] = unit[g] - mult[g] * pivot_row
            scale = [jnp.sqrt(part) for part in inverse]
            inside = (lane >= first) & (lane < first + PIVOTS)
            for g in range(groups):
                where = slice(top + 8 * g, top + 8 * g + 8)
                line = slice(top - shift + 8 * g, top - shift + 8 * g + 8)
                for c in range(chunks):
                    cut = slice(TILE * c, TILE * (c + 1))
                    if c < p:
                        upper[line, cut] = jnp.zeros((8, TILE), F32)
                    elif c == p:
                        upper[line, cut] = jnp.where(
                            lane >= first + 8 * g + row, rows[g][c] * scale[g], 0.0
                        )
                    else:
                        upper[line, cut] = rows[g][c] * scale[g]
                    if c >= p:
                        scaled[first + 8 * g : first + 8 * g + 8, cut] = rows[g][c] * inverse[g]
                    work[where, cut] = jnp.where(inside, unit[g], rows[g][c]) if c == p else rows[g][c]
                scale_blocks.append(scale[g])
            end = first + PIVOTS
            if end < TILE:
                left = left_parts(jnp.concatenate([rows[g][p] * inverse[g] for g in range(groups)]))
                wide = lax.broadcasted_iota(jnp.int32, (TILE - end, TILE), 1)
                for cuts in ([p], [c for c in range(chunks) if c != p]):
                    right = [work[top : top + PIVOTS, TILE * c : TILE * (c + 1)] for c in cuts]
                    change = contract_rows(left, right_parts(jnp.concatenate(right, axis=1)))
                    for at, c in enumerate(cuts):
                        cut = slice(TILE * c, TILE * (c + 1))
                        old = work[base + end : base + TILE, cut]
                        if c == p:
                            old = jnp.where((wide >= first) & (wide < end), 0.0, old)
                        work[base + end : base + TILE, cut] = old - change[end:, TILE * at : TILE * (at + 1)]
        block_lane = lax.broadcasted_iota(jnp.int32, (TILE, TILE), 1)
        block_row = lax.broadcasted_iota(jnp.int32, (TILE, TILE), 0)
        own = slice(base, base + TILE)
        work[own, own] = jnp.where(block_lane <= block_row, work[own, own], 0.0)
        if p + 1 < chunks:
            left = left_parts(scaled[:, base + TILE :])
            right = right_parts(work[own, :])
        for i in range(p + 1, chunks):
            below = slice(TILE * i, TILE * (i + 1))
            part = left[:, TILE * (i - p - 1) : TILE * (i - p)]
            gram_part = contract_rows(part, right[:, TILE * i :])
            work[below, TILE * i :] = work[below, TILE * i :] - gram_part
            inverse_part = contract_rows(part, right[:, : base + TILE])
            if p:
                work[below, :base] = work[below, :base] - inverse_part[:, :base]
            work[below, own] = -inverse_part[:, base:]
        for g, scale in enumerate(scale_blocks):
            where = slice(base + 8 * g, base + 8 * g + 8)
            for c in range(p + 1):
                cut = slice(TILE * c, TILE * (c + 1))
                work[where, cut] = work[where, cut] * scale
        after(p)


def early_kernel(side_ref, member_ref, beside_ref, mine_ref, other_ref, work, upper, scaled, blocks, *, total):
    modes = work.shape[0]
    chunks = modes // TILE
    half = blocks.shape[0] // 2
    piece = half // 4
    sides = ((mine_ref, side_ref[0], member_ref[0]), (other_ref, 1 - side_ref[0], beside_ref[0]))
    for part_ref, side, member in sides:
        for step in range(4):
            at = pl.multiple_of(half * side + piece * (member ^ step), 8)
            blocks[pl.ds(at, piece), :] = part_ref[piece * step : piece * (step + 1), :] * (1.0 / total)
    places, guests = packed_blocks(chunks)
    for at, (p, c) in enumerate(places):
        work[TILE * p : TILE * (p + 1), TILE * c : TILE * (c + 1)] = blocks[TILE * at : TILE * (at + 1), :]
    edge = TILE // 2
    lane = lax.broadcasted_iota(jnp.int32, (edge, TILE), 1)
    corners = {}
    for p, guest in guests.items():
        at = TILE * places.index((p, p)) + edge
        corners[guest] = blocks[at : at + edge, :]
    for guest in sorted({guest for guest, _ in corners}):
        top, cut = TILE * guest, slice(TILE * guest, TILE * (guest + 1))
        work[top : top + edge, cut] = jnp.where(
            lane < edge, corners[guest, 0], pltpu.roll(corners[guest, 1], edge, 1)
        )
        work[top + edge : top + TILE, cut] = jnp.where(lane < edge, 0.0, pltpu.roll(corners[guest, 2], edge, 1))
    factor_blocks(work, scaled, upper, range(chunks // 2), lambda p: None)


def early_panels(side, member, beside, mine, other, modes, total):
    height = TILE * len(packed_blocks(modes // TILE)[0])
    smem, vmem = (pl.BlockSpec(memory_space=space) for space in (pltpu.SMEM, pltpu.VMEM))
    return pl.pallas_call(
        lambda *refs: early_kernel(*refs, total=total),
        out_shape=(
            jax.ShapeDtypeStruct((modes, modes), F32),
            jax.ShapeDtypeStruct((modes // TILE // 2 * TILE, modes), F32),
        ),
        in_specs=[smem, smem, smem, vmem, vmem],
        scratch_shapes=[pltpu.VMEM((TILE, modes), F32), pltpu.VMEM((height, TILE), F32)],
        cost_estimate=pl.CostEstimate(
            flops=16 * modes**3, bytes_accessed=8 * modes * modes, transcendentals=modes
        ),
        compiler_params=pltpu.CompilerParams(vmem_limit_bytes=8 << 20),
        name="early",
    )(side.reshape(1), member.reshape(1), beside.reshape(1), mine, other)


def late_kernel(
    early_ref, early_upper_ref, rows_ref, inverse_ref, modes_hbm, factor_hbm, scaled, upper, solved, sent
):
    modes = inverse_ref.shape[0]
    chunks = modes // TILE
    above = early_upper_ref.shape[0]
    copies = [pltpu.make_async_copy(early_upper_ref, factor_hbm.at[:above, :modes], sent.at[chunks])]
    copies[0].start()
    inverse_ref[...] = early_ref[...]

    upper[modes - above : modes - above + 1, :] = jnp.zeros((1, modes), F32)

    def solve(p):
        own = slice(TILE * p, TILE * (p + 1))
        if TILE * p >= above:
            end = TILE * (p + 1) + (p == chunks - 1)
            lines = upper.at[TILE * p - above : end - above, :]
            copy = pltpu.make_async_copy(lines, factor_hbm.at[TILE * p : end, :modes], sent.at[chunks + p])
            copy.start()
            copies.append(copy)
        width = TILE * (p + 1)
        known = inverse_ref[own, :width]
        first = known.astype(BF16)
        second = (known - first.astype(F32)).astype(BF16)
        left = rows_ref[:, :width]
        solved[p] = (contract_lanes(left, first) + contract_lanes(left, second)).astype(BF16)
        copy = pltpu.make_async_copy(solved.at[p], modes_hbm.at[:, own], sent.at[p])
        copy.start()
        copies.append(copy)

    for p in range(chunks // 2):
        solve(p)
    factor_blocks(inverse_ref, scaled, upper, range(chunks // 2, chunks), solve)
    for copy in copies:
        copy.wait()


def late_panels(early, early_upper, rows):
    count, modes = rows.shape
    chunks = modes // TILE
    vmem, hbm = (pl.BlockSpec(memory_space=space) for space in (pltpu.VMEM, pltpu.HBM))
    return pl.pallas_call(
        late_kernel,
        out_shape=(
            jax.ShapeDtypeStruct((modes, modes), F32),
            jax.ShapeDtypeStruct((count, modes), BF16),
            jax.ShapeDtypeStruct((modes + 1, modes + 1), F32),
        ),
        out_specs=(vmem, hbm, hbm),
        scratch_shapes=[
            pltpu.VMEM((TILE, modes), F32),
            pltpu.VMEM((modes + 1 - early_upper.shape[0], modes), F32),
            pltpu.VMEM((chunks, count, TILE), BF16),
            pltpu.SemaphoreType.DMA((2 * chunks,)),
        ],
        cost_estimate=pl.CostEstimate(
            flops=16 * modes**3, bytes_accessed=8 * modes * modes, transcendentals=modes
        ),
        compiler_params=pltpu.CompilerParams(vmem_limit_bytes=10 << 20),
        name="late",
    )(early, early_upper, rows)


def finish_kernel(inverse_ref, sums_ref, fresh_ref, rows_ref, _, mode_ref, column_ref, *, total):
    modes = inverse_ref.shape[0]
    chunks = modes // TILE
    sums = sums_ref[...] * (1.0 / total)
    cross = [sums[c : c + 1, :] for c in range(chunks)]
    square = sums[chunks : chunks + 1, :]
    norm = jnp.zeros((1, TILE), F32)
    back = [jnp.zeros((1, TILE), F32)] * chunks
    for p in range(chunks):
        own = slice(TILE * p, TILE * (p + 1))
        known = [inverse_ref[own, TILE * c : TILE * (c + 1)] for c in range(p + 1)]
        column = sum(known[c] * cross[c] for c in range(p + 1))
        column = jnp.broadcast_to(jnp.sum(column, axis=1, keepdims=True), (TILE, TILE))
        column_ref[own, :] = column
        norm = norm + jnp.sum(column * column, axis=0, keepdims=True)
        for c in range(p + 1):
            back[c] = back[c] + jnp.sum(known[c] * column, axis=0, keepdims=True)
    last = jnp.sqrt(square - norm)
    share = jnp.concatenate(back, axis=1)
    first = share.astype(BF16)
    second = (share - first.astype(F32)).astype(BF16)
    both = jnp.concatenate([jnp.broadcast_to(part, (16, modes)) for part in (first, second)])
    points = fresh_ref.shape[1]
    for i in range(fresh_ref.shape[0]):
        left = rows_ref[points * i : points * (i + 1), :]
        covered = contract_lanes(both, left)
        covered = covered[:1, :] + covered[16:17, :]
        mode_ref[:, points * i : points * (i + 1)] = (fresh_ref[i : i + 1, :] - covered) / last
    column_ref[modes : modes + 1, :] = last


def finish(inverse, sums, fresh, rows, factor, total):
    count, modes = rows.shape
    vmem, hbm = (pl.BlockSpec(memory_space=space) for space in (pltpu.VMEM, pltpu.HBM))
    return pl.pallas_call(
        lambda *refs: finish_kernel(*refs, total=total),
        grid=(1,),
        out_shape=(
            jax.ShapeDtypeStruct((1, count), F32),
            jax.ShapeDtypeStruct((modes + 1, modes + 1), F32),
        ),
        in_specs=[vmem, vmem, vmem, vmem, hbm],
        out_specs=(
            pl.BlockSpec((1, count), lambda i: (0, 0)),
            pl.BlockSpec((modes + 1, TILE), lambda i: (0, modes // TILE)),
        ),
        input_output_aliases={4: 1},
        cost_estimate=pl.CostEstimate(
            flops=64 * modes * modes, bytes_accessed=4 * modes * modes, transcendentals=0
        ),
        compiler_params=pltpu.CompilerParams(vmem_limit_bytes=8 << 20),
        name="finish",
    )(inverse, sums, fresh, rows, factor)


def local(snapshot, basis, taps):
    modes = basis.shape[-1]
    rows = basis.reshape(-1, modes)
    total = rows.shape[0] * lax.axis_size("gx") * lax.axis_size("gy")
    side = lax.axis_index("gy") & 1
    place = lax.axis_index("gx")
    inner, group = place & 3, (place >> 2) & 3
    slabs = lax.axis_size("gx")
    near_steps, far_steps, *others = bit_groups(slabs)
    even = side == 0
    member, beside = jnp.where(even, inner, group), jnp.where(even, group, inner)
    ways = (tuple(zip(near_steps, far_steps)), tuple(zip(far_steps, near_steps)))

    parts = local_filter(taps, snapshot)
    side, parts = lax.optimization_barrier((side, parts))
    parts = along_slabs_y(parts)
    away = swap(half_gram(1 - side, rows), "gy", 1)
    half = half_gram(side, rows) + away
    bit = 2
    while bit < lax.axis_size("gy"):
        half = half + swap(half, "gy", bit)
        bit *= 2

    piece = half.shape[0] // 4
    height = parts.shape[0] // 3
    quarters = half.reshape(4, piece, TILE)

    def quarter_of(index):
        return lax.dynamic_index_in_dim(quarters, index, 0, keepdims=False)

    before, own, after = parts[:height], parts[height : 2 * height], parts[2 * height :]
    odd = (inner & 1) == 1
    outer = (inner == 0) | (inner == 3)
    by_one, by_three = jnp.where(odd, before, after), jnp.where(odd, after, before)
    over = jnp.where(inner == 0, before, after)
    wanted = jnp.where((inner == 0) == even, group - 1, group + 1) & 3
    next_group = (group ^ wanted) == 1

    def exchanged(blocks, riders, way):
        return [
            swap_by_side(block if rider is None else jnp.concatenate([block, rider]), steps)
            for block, rider, steps in zip(blocks, riders, way)
        ]

    got = exchanged(
        [quarter_of(member ^ step) for step in (1, 2, 3)],
        (jnp.where(even, by_one, over), None, jnp.where(even, by_three, over)),
        ways[0],
    )
    quarter = sum([block[:piece] for block in got], quarter_of(member))
    one, three = got[0][piece:], got[2][piece:]

    crossed = jnp.where(outer, jnp.where(next_group, one, three), by_three)
    riders = (jnp.where(even, three, by_one), None, jnp.where(even, three, crossed))
    got = exchanged([quarter] * 3, riders, ways[1])
    quarter = sum([block[:piece] for block in got], quarter)
    if slabs == 16:
        last_one, last_three = got[0][piece:], got[2][piece:]
        near = jnp.where(even, one, last_one)
        passed = jnp.where(outer, jnp.where(next_group, last_one, last_three), three)
        far = jnp.where(even, passed, last_three)
    else:
        for steps in others:
            quarter = sum([swap(quarter, "gx", step) for step in steps], quarter)
        forward = [(i, (i + 1) % slabs) for i in range(slabs)]
        near = lax.ppermute(after, "gx", forward)
        far = lax.ppermute(before, "gx", [(j, i) for i, j in forward])

    fresh, cross = local_cross(own, near, far, rows)
    block = jnp.concatenate([quarter, cross])
    gathered = [block] + exchanged([block] * 3, (None,) * 3, ways[0])
    sums = sum([got[piece:] for got in gathered[1:]], block[piece:])
    mine = jnp.concatenate([got[:piece] for got in gathered])
    other = swap(mine, "gy", 1)
    sums = sums + swap_by_side(sums, ways[1][0])
    for steps in others:
        sums = sum([swap(sums, "gx", step) for step in steps], sums)
    bit = 2
    while bit < lax.axis_size("gy"):
        sums = sums + swap(sums, "gy", bit)
        bit *= 2
    hopped = swap_by_side(sums, ways[1][1])
    sums = sums + hopped
    early, early_upper = early_panels(side, member, beside, mine, other, modes, total)
    sums, early = lax.optimization_barrier((sums, early))
    sums = sums + swap(sums, "gy", 1)
    inverse, new_modes, factor = late_panels(early, early_upper, rows)
    new_mode, factor = finish(inverse, sums, fresh, rows, factor, total)
    return (new_modes.reshape(basis.shape), new_mode.reshape(basis.shape[:-1]), factor)


def solution(mesh):
    in_specs = (P(None, "gx", "gy", None), P(None, "gx", "gy", None, None), P())
    out_specs = (P(None, "gx", "gy", None, None), P(None, "gx", "gy", None), P())

    return jax.shard_map(local, mesh=mesh, in_specs=in_specs, out_specs=out_specs, check_vma=False)
```

```python
import jax
import jax.numpy as jnp
from jax import lax
from jax.experimental import pallas as pl
from jax.experimental.pallas import tpu as pltpu
from jax.sharding import PartitionSpec as P


STRIDE = 8
TILE = 128
PIVOTS = 32
F32 = jnp.float32
BF16 = jnp.bfloat16
HIGHEST = lax.Precision.HIGHEST


def swap(block, axis, step):
    return lax.ppermute(block, axis, [(i, i ^ step) for i in range(lax.axis_size(axis))])


def swap_by_side(block, steps):
    wide = lax.axis_size("gy")
    pairs = [
        (i * wide + j, (i ^ steps[j & 1]) * wide + j) for i in range(lax.axis_size("gx")) for j in range(wide)
    ]
    return lax.ppermute(block, ("gx", "gy"), pairs)


def bit_groups(size):
    groups, bit = [], 1
    while bit < size:
        groups.append((bit, 2 * bit, 3 * bit) if 4 * bit <= size else (bit,))
        bit *= 4 if 4 * bit <= size else 2
    return groups


def contract_rows(a, b, precision=None):
    return lax.dot_general(
        a, b, (((0,), (0,)), ((), ())), precision=precision, preferred_element_type=F32
    )


def contract_lanes(a, b, precision=None):
    return lax.dot_general(
        a, b, (((1,), (1,)), ((), ())), precision=precision, preferred_element_type=F32
    )


def packed_blocks(chunks):
    whole = chunks - chunks // 4
    blocks = [(p, c) for p in range(chunks) for c in range(p, chunks) if p < c or p < whole]
    guests = {i: (whole + i // 3, i % 3) for i in range(3 * (chunks // 4))}
    return blocks, guests


def gram_kernel(side_ref, rows_ref, out_ref):
    blocks, guests = packed_blocks(rows_ref.shape[1] // TILE)
    half, edge = out_ref.shape[0], TILE // 2
    lane = lax.broadcasted_iota(jnp.int32, (edge, TILE), 1)
    for side in range(2):

        @pl.when(side_ref[0] == side)
        def _():
            tops = range(half * side, half * (side + 1), edge)
            panels = {}
            for p in sorted({blocks[top // TILE][0] for top in tops}):
                last = max(blocks[top // TILE][1] for top in tops if blocks[top // TILE][0] == p)
                panels[p] = contract_rows(
                    rows_ref[:, TILE * p : TILE * (p + 1)], rows_ref[:, TILE * p : TILE * (last + 1)]
                )
            for top in tops:
                p, c = blocks[top // TILE]
                low = top % TILE
                value = panels[p][low : low + edge, TILE * (c - p) : TILE * (c - p + 1)]
                if p == c and low and p in guests:
                    guest, quarter = guests[p]
                    if guest not in panels:
                        own = rows_ref[:, TILE * guest : TILE * (guest + 1)]
                        panels[guest] = contract_rows(own, own)
                    part = panels[guest][edge:, :TILE] if quarter == 2 else panels[guest][:edge, :TILE]
                    value = jnp.where(lane < edge, pltpu.roll(part, edge, 1) if quarter else part, value)
                out_ref[top - half * side : top - half * side + edge, :] = value


def half_gram(side, rows):
    count, modes = rows.shape
    height = TILE * len(packed_blocks(modes // TILE)[0]) // 2
    return pl.pallas_call(
        gram_kernel,
        out_shape=jax.ShapeDtypeStruct((height, TILE), F32),
        in_specs=[pl.BlockSpec(memory_space=pltpu.SMEM), pl.BlockSpec(memory_space=pltpu.VMEM)],
        cost_estimate=pl.CostEstimate(
            flops=2 * count * height * TILE, bytes_accessed=4 * height * TILE, transcendentals=0
        ),
        compiler_params=pltpu.CompilerParams(vmem_limit_bytes=4 << 20),
        name="gram",
    )(side.reshape(1), rows)


def weights(taps_ref, direction, lag):
    line = taps_ref[...].astype(F32)[direction : direction + 1, :]
    found = jnp.zeros(lag.shape, F32)
    for tap in range(2 * STRIDE + 1):
        value = jnp.broadcast_to(line[:, tap : tap + 1], (1, lag.shape[1]))
        found = jnp.where(lag == tap, value, found)
    return found


def parted(index, size, bound):
    if size & (size - 1) == 0:
        return index >> (size.bit_length() - 1), index & (size - 1)
    scale = -(-(1 << 16) // size)
    assert all((i * scale) >> 16 == i // size for i in range(bound))
    quotient = (index * scale) >> 16
    return quotient, index - size * quotient


def filter_kernel(taps_hbm, cells_hbm, out_ref, taps_ref, band, cells, arrived, *, cells_x, cells_y):
    taps_copy = pltpu.make_async_copy(taps_hbm, taps_ref, arrived.at[0])
    cells_copy = pltpu.make_async_copy(cells_hbm, cells, arrived.at[1])
    taps_copy.start()
    cells_copy.start()
    depth, points = band.shape
    height = out_ref.shape[0]
    z = lax.broadcasted_iota(jnp.int32, (TILE, points), 0)
    p = lax.broadcasted_iota(jnp.int32, (TILE, points), 1)
    lag = z - STRIDE * p + STRIDE
    taps_copy.wait()
    pattern = weights(taps_ref, 2, jnp.where(lag < 0, lag + depth, lag))
    for block in range(depth // TILE):
        turned = pltpu.roll(pattern, TILE // STRIDE * block, 1) if block else pattern
        band[TILE * block : TILE * (block + 1), :] = turned.astype(BF16)
    count = cells.shape[0]
    per_y = cells_y // STRIDE
    out = lax.broadcasted_iota(jnp.int32, (height, count), 0)
    cell = lax.broadcasted_iota(jnp.int32, (height, count), 1)
    slot, within = parted(out, height // 9, height)
    kind, r = parted(slot, 3, 9)
    comp, q = parted(within, per_y, height // 9)
    rest, y = parted(cell, cells_y, count)
    cell_comp, x = parted(rest, cells_x, count)
    y = y + jnp.where(kind == 1, -cells_y, jnp.where(kind == 2, cells_y, 0))
    weight = weights(taps_ref, 0, x - STRIDE * (r - 1) + STRIDE)
    weight = weight * weights(taps_ref, 1, y - STRIDE * q + STRIDE)
    weight = jnp.where(cell_comp == comp, weight, 0.0)
    cells_copy.wait()
    along_z = jnp.dot(cells[...], band[...], preferred_element_type=F32)
    out_ref[...] = jnp.dot(weight, along_z, precision=HIGHEST, preferred_element_type=F32)


def local_filter(taps, snapshot):
    comps, cells_x, cells_y, cells_z = snapshot.shape
    assert cells_x == STRIDE
    points = cells_z // STRIDE
    height = 9 * padded_rows(comps * cells_y // STRIDE)
    cells = snapshot.reshape(-1, cells_z)
    return pl.pallas_call(
        lambda *refs: filter_kernel(*refs, cells_x=cells_x, cells_y=cells_y),
        out_shape=jax.ShapeDtypeStruct((height, points), F32),
        in_specs=[pl.BlockSpec(memory_space=pltpu.HBM)] * 2,
        scratch_shapes=[
            pltpu.VMEM(taps.shape, BF16),
            pltpu.VMEM((cells_z, points), BF16),
            pltpu.VMEM(cells.shape, BF16),
            pltpu.SemaphoreType.DMA((2,)),
        ],
        cost_estimate=pl.CostEstimate(
            flops=4 * cells.size * points, bytes_accessed=2 * cells.size, transcendentals=0
        ),
        compiler_params=pltpu.CompilerParams(vmem_limit_bytes=4 << 20),
        name="filter",
    )(*(pltpu.with_memory_space_constraint(array, pltpu.HBM) for array in (taps, cells)))


def padded_rows(rows):
    return -(-rows // 8) * 8


def along_slabs_y(parts):
    height = parts.shape[0] // 3
    own, up, down = parts[:height], parts[height : 2 * height], parts[2 * height :]
    count = lax.axis_size("gy")
    if count == 2:
        return own + swap(jnp.where(lax.axis_index("gy") == 1, down, up), "gy", 1)
    pairs = [(i, i + 1) for i in range(count - 1)]
    low = lax.ppermute(up, "gy", pairs)
    return own + low + lax.ppermute(down, "gy", [(j, i) for i, j in pairs])


def cross_kernel(own_ref, low_ref, high_ref, rows_ref, fresh_ref, out_ref):
    lines, points = fresh_ref.shape
    modes = rows_ref.shape[1]
    fresh = (own_ref[...] + low_ref[...] + high_ref[...]).astype(BF16).astype(F32)
    fresh_ref[...] = fresh[:lines, :]
    total = jnp.zeros((8, modes), F32)
    square = jnp.zeros((1, 1), F32)
    for i in range(lines):
        line = fresh[i : i + 1, :]
        square = square + jnp.sum(line * line, axis=1, keepdims=True)
        left = jnp.broadcast_to(line, (8, points)).astype(BF16)
        total = total + jnp.dot(
            left, rows_ref[points * i : points * (i + 1), :], preferred_element_type=F32
        )
    out_ref[...] = jnp.zeros(out_ref.shape, F32)
    for c in range(modes // TILE):
        out_ref[c : c + 1, :] = total[:1, TILE * c : TILE * (c + 1)]
    out_ref[modes // TILE : modes // TILE + 1, :] = jnp.broadcast_to(square, (1, TILE))


def local_cross(own, low, high, rows):
    points = own.shape[1]
    return pl.pallas_call(
        cross_kernel,
        out_shape=(
            jax.ShapeDtypeStruct((rows.shape[0] // points, points), F32),
            jax.ShapeDtypeStruct((padded_rows(rows.shape[1] // TILE + 1), TILE), F32),
        ),
        cost_estimate=pl.CostEstimate(flops=16 * rows.size, bytes_accessed=2 * rows.size, transcendentals=0),
        compiler_params=pltpu.CompilerParams(vmem_limit_bytes=4 << 20),
        name="cross",
    )(own, low, high, rows)


def split(value):
    parts = []
    for _ in range(3):
        parts.append(value.astype(BF16))
        value = value - parts[-1].astype(F32)
    return parts


def left_parts(value):
    a, b, c = split(value)
    return jnp.concatenate([a, a, b, b, a, c])


def right_parts(value):
    a, b, c = split(value)
    return jnp.concatenate([a, b, a, b, c, a])


def factor_blocks(work, scaled, upper, panels, after):
    modes = work.shape[0]
    chunks = modes // TILE
    groups = PIVOTS // 8
    lane = lax.broadcasted_iota(jnp.int32, (8, TILE), 1)
    row = lax.broadcasted_iota(jnp.int32, (8, TILE), 0)
    for p in panels:
        base = p * TILE
        shift = panels[0] * TILE
        scale_blocks = []
        for j in range(TILE // PIVOTS):
            first = PIVOTS * j
            top = base + first
            rows = [
                [work[top + 8 * g : top + 8 * g + 8, TILE * c : TILE * (c + 1)] for c in range(chunks)]
                for g in range(groups)
            ]
            cols = [
                [
                    jnp.broadcast_to(rows[g][p][:, first + k : first + k + 1], (8, TILE))
                    if g >= k // 8
                    else None
                    for g in range(groups)
                ]
                for k in range(PIVOTS)
            ]
            unit = [jnp.where(lane == first + 8 * g + row, 1.0, 0.0).astype(F32) for g in range(groups)]
            inverse = [jnp.zeros((8, TILE), F32) for _ in range(groups)]
            for k in range(PIVOTS):
                own, sub = k // 8, k % 8
                pivot = cols[k][own][sub : sub + 1, :]
                recip = 1.0 / pivot
                inverse[own] = jnp.where(row == sub, recip, inverse[own])
                mult = {g: cols[k][g] * recip for g in range(own, groups)}
                for later in range(k + 1, PIVOTS):
                    factor = cols[k][later // 8][later % 8 : later % 8 + 1, :]
                    for g in range(later // 8, groups):
                        cols[later][g] = cols[later][g] - mult[g] * factor
                mult[own] = jnp.where(row > sub, mult[own], 0.0)
                below = range(own + (sub == 7), groups)
                for c in range(chunks):
                    pivot_row = rows[own][c][sub : sub + 1, :]
                    for g in below:
                        rows[g][c] = rows[g][c] - mult[g] * pivot_row
                pivot_row = unit[own][sub : sub + 1, :]
                for g in below:
                    unit[g] = unit[g] - mult[g] * pivot_row
            scale = [jnp.sqrt(part) for part in inverse]
            inside = (lane >= first) & (lane < first + PIVOTS)
            for g in range(groups):
                where = slice(top + 8 * g, top + 8 * g + 8)
                line = slice(top - shift + 8 * g, top - shift + 8 * g + 8)
                for c in range(chunks):
                    cut = slice(TILE * c, TILE * (c + 1))
                    if c < p:
                        upper[line, cut] = jnp.zeros((8, TILE), F32)
                    elif c == p:
                        upper[line, cut] = jnp.where(
                            lane >= first + 8 * g + row, rows[g][c] * scale[g], 0.0
                        )
                    else:
                        upper[line, cut] = rows[g][c] * scale[g]
                    if c >= p:
                        scaled[first + 8 * g : first + 8 * g + 8, cut] = rows[g][c] * inverse[g]
                    work[where, cut] = jnp.where(inside, unit[g], rows[g][c]) if c == p else rows[g][c]
                scale_blocks.append(scale[g])
            end = first + PIVOTS
            if end < TILE:
                left = left_parts(jnp.concatenate([rows[g][p] * inverse[g] for g in range(groups)]))
                wide = lax.broadcasted_iota(jnp.int32, (TILE - end, TILE), 1)
                for cuts in ([p], [c for c in range(chunks) if c != p]):
                    right = [work[top : top + PIVOTS, TILE * c : TILE * (c + 1)] for c in cuts]
                    change = contract_rows(left, right_parts(jnp.concatenate(right, axis=1)))
                    for at, c in enumerate(cuts):
                        cut = slice(TILE * c, TILE * (c + 1))
                        old = work[base + end : base + TILE, cut]
                        if c == p:
                            old = jnp.where((wide >= first) & (wide < end), 0.0, old)
                        work[base + end : base + TILE, cut] = old - change[end:, TILE * at : TILE * (at + 1)]
        block_lane = lax.broadcasted_iota(jnp.int32, (TILE, TILE), 1)
        block_row = lax.broadcasted_iota(jnp.int32, (TILE, TILE), 0)
        own = slice(base, base + TILE)
        work[own, own] = jnp.where(block_lane <= block_row, work[own, own], 0.0)
        if p + 1 < chunks:
            left = left_parts(scaled[:, base + TILE :])
            right = right_parts(work[own, :])
        for i in range(p + 1, chunks):
            below = slice(TILE * i, TILE * (i + 1))
            part = left[:, TILE * (i - p - 1) : TILE * (i - p)]
            gram_part = contract_rows(part, right[:, TILE * i :])
            work[below, TILE * i :] = work[below, TILE * i :] - gram_part
            inverse_part = contract_rows(part, right[:, : base + TILE])
            if p:
                work[below, :base] = work[below, :base] - inverse_part[:, :base]
            work[below, own] = -inverse_part[:, base:]
        for g, scale in enumerate(scale_blocks):
            where = slice(base + 8 * g, base + 8 * g + 8)
            for c in range(p + 1):
                cut = slice(TILE * c, TILE * (c + 1))
                work[where, cut] = work[where, cut] * scale
        after(p)


def early_kernel(side_ref, member_ref, beside_ref, mine_ref, other_ref, work, upper, scaled, blocks, *, total):
    modes = work.shape[0]
    chunks = modes // TILE
    half = blocks.shape[0] // 2
    piece = half // 4
    sides = ((mine_ref, side_ref[0], member_ref[0]), (other_ref, 1 - side_ref[0], beside_ref[0]))
    for part_ref, side, member in sides:
        for step in range(4):
            at = pl.multiple_of(half * side + piece * (member ^ step), 8)
            blocks[pl.ds(at, piece), :] = part_ref[piece * step : piece * (step + 1), :] * (1.0 / total)
    places, guests = packed_blocks(chunks)
    for at, (p, c) in enumerate(places):
        work[TILE * p : TILE * (p + 1), TILE * c : TILE * (c + 1)] = blocks[TILE * at : TILE * (at + 1), :]
    edge = TILE // 2
    lane = lax.broadcasted_iota(jnp.int32, (edge, TILE), 1)
    corners = {}
    for p, guest in guests.items():
        at = TILE * places.index((p, p)) + edge
        corners[guest] = blocks[at : at + edge, :]
    for guest in sorted({guest for guest, _ in corners}):
        top, cut = TILE * guest, slice(TILE * guest, TILE * (guest + 1))
        work[top : top + edge, cut] = jnp.where(
            lane < edge, corners[guest, 0], pltpu.roll(corners[guest, 1], edge, 1)
        )
        work[top + edge : top + TILE, cut] = jnp.where(lane < edge, 0.0, pltpu.roll(corners[guest, 2], edge, 1))
    factor_blocks(work, scaled, upper, range(chunks // 2), lambda p: None)


def early_panels(side, member, beside, mine, other, modes, total):
    height = TILE * len(packed_blocks(modes // TILE)[0])
    smem, vmem = (pl.BlockSpec(memory_space=space) for space in (pltpu.SMEM, pltpu.VMEM))
    return pl.pallas_call(
        lambda *refs: early_kernel(*refs, total=total),
        out_shape=(
            jax.ShapeDtypeStruct((modes, modes), F32),
            jax.ShapeDtypeStruct((modes // TILE // 2 * TILE, modes), F32),
        ),
        in_specs=[smem, smem, smem, vmem, vmem],
        scratch_shapes=[pltpu.VMEM((TILE, modes), F32), pltpu.VMEM((height, TILE), F32)],
        cost_estimate=pl.CostEstimate(
            flops=16 * modes**3, bytes_accessed=8 * modes * modes, transcendentals=modes
        ),
        compiler_params=pltpu.CompilerParams(vmem_limit_bytes=8 << 20),
        name="early",
    )(side.reshape(1), member.reshape(1), beside.reshape(1), mine, other)


def late_kernel(
    early_ref, early_upper_ref, rows_ref, inverse_ref, modes_hbm, factor_hbm, scaled, upper, solved, sent
):
    modes = inverse_ref.shape[0]
    chunks = modes // TILE
    above = early_upper_ref.shape[0]
    copies = [pltpu.make_async_copy(early_upper_ref, factor_hbm.at[:above, :modes], sent.at[chunks])]
    copies[0].start()
    inverse_ref[...] = early_ref[...]

    upper[modes - above : modes - above + 1, :] = jnp.zeros((1, modes), F32)

    def solve(p):
        own = slice(TILE * p, TILE * (p + 1))
        if TILE * p >= above:
            end = TILE * (p + 1) + (p == chunks - 1)
            lines = upper.at[TILE * p - above : end - above, :]
            copy = pltpu.make_async_copy(lines, factor_hbm.at[TILE * p : end, :modes], sent.at[chunks + p])
            copy.start()
            copies.append(copy)
        width = TILE * (p + 1)
        known = inverse_ref[own, :width]
        first = known.astype(BF16)
        second = (known - first.astype(F32)).astype(BF16)
        left = rows_ref[:, :width]
        solved[p] = (contract_lanes(left, first) + contract_lanes(left, second)).astype(BF16)
        copy = pltpu.make_async_copy(solved.at[p], modes_hbm.at[:, own], sent.at[p])
        copy.start()
        copies.append(copy)

    for p in range(chunks // 2):
        solve(p)
    factor_blocks(inverse_ref, scaled, upper, range(chunks // 2, chunks), solve)
    for copy in copies:
        copy.wait()


def late_panels(early, early_upper, rows):
    count, modes = rows.shape
    chunks = modes // TILE
    vmem, hbm = (pl.BlockSpec(memory_space=space) for space in (pltpu.VMEM, pltpu.HBM))
    return pl.pallas_call(
        late_kernel,
        out_shape=(
            jax.ShapeDtypeStruct((modes, modes), F32),
            jax.ShapeDtypeStruct((count, modes), BF16),
            jax.ShapeDtypeStruct((modes + 1, modes + 1), F32),
        ),
        out_specs=(vmem, hbm, hbm),
        scratch_shapes=[
            pltpu.VMEM((TILE, modes), F32),
            pltpu.VMEM((modes + 1 - early_upper.shape[0], modes), F32),
            pltpu.VMEM((chunks, count, TILE), BF16),
            pltpu.SemaphoreType.DMA((2 * chunks,)),
        ],
        cost_estimate=pl.CostEstimate(
            flops=16 * modes**3, bytes_accessed=8 * modes * modes, transcendentals=modes
        ),
        compiler_params=pltpu.CompilerParams(vmem_limit_bytes=10 << 20),
        name="late",
    )(early, early_upper, rows)


def finish_kernel(inverse_ref, sums_ref, fresh_ref, rows_ref, _, mode_ref, column_ref, *, total):
    modes = inverse_ref.shape[0]
    chunks = modes // TILE
    sums = sums_ref[...] * (1.0 / total)
    cross = [sums[c : c + 1, :] for c in range(chunks)]
    square = sums[chunks : chunks + 1, :]
    norm = jnp.zeros((1, TILE), F32)
    back = [jnp.zeros((1, TILE), F32)] * chunks
    for p in range(chunks):
        own = slice(TILE * p, TILE * (p + 1))
        known = [inverse_ref[own, TILE * c : TILE * (c + 1)] for c in range(p + 1)]
        column = sum(known[c] * cross[c] for c in range(p + 1))
        column = jnp.broadcast_to(jnp.sum(column, axis=1, keepdims=True), (TILE, TILE))
        column_ref[own, :] = column
        norm = norm + jnp.sum(column * column, axis=0, keepdims=True)
        for c in range(p + 1):
            back[c] = back[c] + jnp.sum(known[c] * column, axis=0, keepdims=True)
    last = jnp.sqrt(square - norm)
    share = jnp.concatenate(back, axis=1)
    first = share.astype(BF16)
    second = (share - first.astype(F32)).astype(BF16)
    both = jnp.concatenate([jnp.broadcast_to(part, (16, modes)) for part in (first, second)])
    points = fresh_ref.shape[1]
    for i in range(fresh_ref.shape[0]):
        left = rows_ref[points * i : points * (i + 1), :]
        covered = contract_lanes(both, left)
        covered = covered[:1, :] + covered[16:17, :]
        mode_ref[:, points * i : points * (i + 1)] = (fresh_ref[i : i + 1, :] - covered) / last
    column_ref[modes : modes + 1, :] = last


def finish(inverse, sums, fresh, rows, factor, total):
    count, modes = rows.shape
    vmem, hbm = (pl.BlockSpec(memory_space=space) for space in (pltpu.VMEM, pltpu.HBM))
    return pl.pallas_call(
        lambda *refs: finish_kernel(*refs, total=total),
        grid=(1,),
        out_shape=(
            jax.ShapeDtypeStruct((1, count), F32),
            jax.ShapeDtypeStruct((modes + 1, modes + 1), F32),
        ),
        in_specs=[vmem, vmem, vmem, vmem, hbm],
        out_specs=(
            pl.BlockSpec((1, count), lambda i: (0, 0)),
            pl.BlockSpec((modes + 1, TILE), lambda i: (0, modes // TILE)),
        ),
        input_output_aliases={4: 1},
        cost_estimate=pl.CostEstimate(
            flops=64 * modes * modes, bytes_accessed=4 * modes * modes, transcendentals=0
        ),
        compiler_params=pltpu.CompilerParams(vmem_limit_bytes=8 << 20),
        name="finish",
    )(inverse, sums, fresh, rows, factor)


def local(snapshot, basis, taps):
    modes = basis.shape[-1]
    rows = basis.reshape(-1, modes)
    total = rows.shape[0] * lax.axis_size("gx") * lax.axis_size("gy")
    side = lax.axis_index("gy") & 1
    place = lax.axis_index("gx")
    inner, group = place & 3, (place >> 2) & 3
    slabs = lax.axis_size("gx")
    near_steps, far_steps, *others = bit_groups(slabs)
    even = side == 0
    member, beside = jnp.where(even, inner, group), jnp.where(even, group, inner)
    ways = (tuple(zip(near_steps, far_steps)), tuple(zip(far_steps, near_steps)))

    parts = local_filter(taps, snapshot)
    side, parts = lax.optimization_barrier((side, parts))
    parts = along_slabs_y(parts)
    away = swap(half_gram(1 - side, rows), "gy", 1)
    half = half_gram(side, rows) + away
    bit = 2
    while bit < lax.axis_size("gy"):
        half = half + swap(half, "gy", bit)
        bit *= 2

    piece = half.shape[0] // 4
    height = parts.shape[0] // 3
    quarters = half.reshape(4, piece, TILE)

    def quarter_of(index):
        return lax.dynamic_index_in_dim(quarters, index, 0, keepdims=False)

    before, own, after = parts[:height], parts[height : 2 * height], parts[2 * height :]
    odd = (inner & 1) == 1
    outer = (inner == 0) | (inner == 3)
    by_one, by_three = jnp.where(odd, before, after), jnp.where(odd, after, before)
    over = jnp.where(inner == 0, before, after)
    wanted = jnp.where((inner == 0) == even, group - 1, group + 1) & 3
    next_group = (group ^ wanted) == 1

    def exchanged(blocks, riders, way):
        return [
            swap_by_side(block if rider is None else jnp.concatenate([block, rider]), steps)
            for block, rider, steps in zip(blocks, riders, way)
        ]

    got = exchanged(
        [quarter_of(member ^ step) for step in (1, 2, 3)],
        (jnp.where(even, by_one, over), None, jnp.where(even, by_three, over)),
        ways[0],
    )
    quarter = sum([block[:piece] for block in got], quarter_of(member))
    one, three = got[0][piece:], got[2][piece:]

    crossed = jnp.where(outer, jnp.where(next_group, one, three), by_three)
    riders = (jnp.where(even, three, by_one), None, jnp.where(even, three, crossed))
    got = exchanged([quarter] * 3, riders, ways[1])
    quarter = sum([block[:piece] for block in got], quarter)
    if slabs == 16:
        last_one, last_three = got[0][piece:], got[2][piece:]
        near = jnp.where(even, one, last_one)
        passed = jnp.where(outer, jnp.where(next_group, last_one, last_three), three)
        far = jnp.where(even, passed, last_three)
    else:
        for steps in others:
            quarter = sum([swap(quarter, "gx", step) for step in steps], quarter)
        forward = [(i, (i + 1) % slabs) for i in range(slabs)]
        near = lax.ppermute(after, "gx", forward)
        far = lax.ppermute(before, "gx", [(j, i) for i, j in forward])

    fresh, cross = local_cross(own, near, far, rows)
    block = jnp.concatenate([quarter, cross])
    gathered = [block] + exchanged([block] * 3, (None,) * 3, ways[0])
    sums = sum([got[piece:] for got in gathered[1:]], block[piece:])
    mine = jnp.concatenate([got[:piece] for got in gathered])
    other = swap(mine, "gy", 1)
    sums = sums + swap_by_side(sums, ways[1][0])
    for steps in others:
        sums = sum([swap(sums, "gx", step) for step in steps], sums)
    bit = 2
    while bit < lax.axis_size("gy"):
        sums = sums + swap(sums, "gy", bit)
        bit *= 2
    hopped = swap_by_side(sums, ways[1][1])
    sums = sums + hopped
    early, early_upper = early_panels(side, member, beside, mine, other, modes, total)
    sums, early = lax.optimization_barrier((sums, early))
    sums = sums + swap(sums, "gy", 1)
    inverse, new_modes, factor = late_panels(early, early_upper, rows)
    new_mode, factor = finish(inverse, sums, fresh, rows, factor, total)
    return (new_modes.reshape(basis.shape), new_mode.reshape(basis.shape[:-1]), factor)


def solution(mesh):
    in_specs = (P(None, "gx", "gy", None), P(None, "gx", "gy", None, None), P())
    out_specs = (P(None, "gx", "gy", None, None), P(None, "gx", "gy", None), P())

    return jax.shard_map(local, mesh=mesh, in_specs=in_specs, out_specs=out_specs, check_vma=False)
```
